32 devices in a mesh: sec: 4 (over x, core), lat: 2 (over y), col: 4 (over z).
Axes of the slice: x: 2, y: 2, z: 4, core: 2. Of those that a mesh axis runs over, the one named last changes fastest.
Arguments:
- state: float32 [1, 4, 28, 192, 384], P(None, 'sec', None, 'lat', 'col'), may hold values from -6 to 6
- forcing: float32 [1, 4, 28, 192, 384], P(None, 'sec', None, 'lat', 'col'), may hold values from -4 to 4
- crm_moisture: bfloat16 [1, 32, 28, 8, 4, 2304], P(None, None, None, ('sec', 'lat'), 'col'), may hold values from -6 to 6
- cloud_order: int32 [4, 2, 9216], P('col', 'lat'), may hold values from 0 to 9215, each once within a row
- wave_table: int32 [128], replicated, may hold values from 0 to 127, each once
Outputs:
- state_out: float32 [1, 4, 28, 192, 384], P(None, 'sec', None, 'lat', 'col')
- spectral: float32 [4, 1, 28, 128, 2, 128], P('sec', None, 'col', 'lat')
The draws below stay inside these ranges and needn't reach their ends.
Inputs may be any that keep to these rules, and one draw needn't show every extreme that they name: `cloud_order`: every row lists each of the 9216 columns of a band block once. `wave_table`: each wavenumber stands in exactly one slot.
All inputs are finite; a program needn't handle non-finite values.
Results may differ from the reference program's by a relative error of at most 0.0003.
Values sent between devices are 32-bit elements; how exact they have to be, the bound alone decides.
A program may use at most 128 MiB of HBM per device.

```python
import math
import jax
import jax.numpy as jnp
from jax import lax

NLON = 384
NLAT = 192
L = 28
F = 4
MMAX = 128
NCRM = 32
NSUB = 4
ENS = 1
LON_BLOCK = 96
BLOCK_COLS = 9216
TARGETS = 8
PER_TARGET = 1152
RUN_COLS = 2304
N_LAT = 2
N_COL = 4


def block_levels(stream_key, dims, shards, least, top_value):
    def one(dim, blocks):
        draws = jax.random.uniform(jax.random.fold_in(jax.random.fold_in(stream_key, 6), dim), (blocks,), jnp.float32, least / len(shards), top_value / len(shards))
        return jnp.repeat(jnp.exp(draws), dims[dim] // blocks).reshape((-1,) + (1,) * (len(dims) - dim - 1))

    level = one(*shards[0])
    for cut in shards[1:]:
        level = level * one(*cut)
    return level


def normal_values(rng, dims, width, reach, shards=(), held_as=jnp.bfloat16):
    factor_of = block_levels(rng, dims, shards, -0.22, 0.18) if shards else 1.0
    values = jax.random.normal(rng, dims, jnp.float32) * width * factor_of
    return jnp.minimum(jnp.maximum(values, -reach), reach).astype(held_as)


def setup_inputs(seed: int = 0) -> dict:
    splits = jax.random.split(jax.random.key(seed), 6)
    state = normal_values(splits[0], (ENS, F, L, NLAT, NLON), 1.0, 6.0, ((1, 4), (3, 2), (4, 4)), jnp.float32)
    forcing = normal_values(splits[1], (ENS, F, L, NLAT, NLON), 0.5, 4.0, ((1, 4), (3, 2), (4, 4)), jnp.float32)
    crm_moisture = normal_values(splits[2], (ENS, NCRM, L, TARGETS, N_COL, RUN_COLS), 1.0, 6.0, ((3, 8), (4, 4)))
    cloud_order = jax.vmap(lambda own: jax.random.permutation(own, BLOCK_COLS))(jax.random.split(splits[3], N_COL * N_LAT)).reshape((N_COL, N_LAT, BLOCK_COLS)).astype(jnp.int32)
    wave_table = jax.random.permutation(splits[4], MMAX).astype(jnp.int32)
    return dict(state=state, forcing=forcing, crm_moisture=crm_moisture, cloud_order=cloud_order, wave_table=wave_table)


COURANT_SCALE = 0.4
CONDENSE = 0.5

def transport(values, courant, mixing):
    forward = jnp.roll(values, -1, axis=0)
    behind = jnp.roll(values, 1, axis=0)
    return -0.5 * courant * (forward - behind) + mixing * (forward - 2.0 * values + behind)

def cloud_model(vertical_state_stack, forcing, vapour_mass_fraction):
    wind_u = vertical_state_stack[0]
    wind_v = vertical_state_stack[1]
    atmospheric_warmth = vertical_state_stack[2]
    humidity = vertical_state_stack[3]
    courant = COURANT_SCALE * jnp.tanh(wind_u)
    mixing = 0.2 + 0.5 * jnp.abs(courant)
    convective_warming_rate = jnp.broadcast_to(atmospheric_warmth, vapour_mass_fraction.shape)
    crm_water = humidity + vapour_mass_fraction
    start_water = crm_water
    ground_precipitation = jnp.zeros_like(atmospheric_warmth)
    for substep in range(NSUB):
        heat_move = transport(convective_warming_rate, courant, mixing)
        water_move = transport(crm_water, courant, mixing)
        condensed = CONDENSE * jnp.maximum(crm_water - convective_warming_rate, 0.0)
        convective_warming_rate = convective_warming_rate + heat_move + condensed + forcing[2] / NSUB
        crm_water = crm_water + water_move - condensed + forcing[3] / NSUB
        ground_precipitation = ground_precipitation + lax.optimization_barrier(jnp.mean(condensed, axis=0))
    ground_precipitation = ground_precipitation / NSUB
    zonal_velocity_rate = -ground_precipitation * wind_u + forcing[0]
    meridional_velocity_rate = -ground_precipitation * wind_v + forcing[1]
    warming_rate_change = lax.optimization_barrier(jnp.mean(convective_warming_rate, axis=0)) - atmospheric_warmth
    vapour_rate_change = lax.optimization_barrier(jnp.mean(crm_water - start_water, axis=0))
    return jnp.stack((zonal_velocity_rate, meridional_velocity_rate, warming_rate_change, vapour_rate_change))

def trig_table(longitudes, wave_numbers):
    phase = (longitudes[:, None] * wave_numbers[None, :] % NLON).astype(jnp.float32) * (2.0 * math.pi / NLON)
    return jnp.stack((jnp.cos(phase), jnp.sin(phase)), axis=1) / math.sqrt(NLON)

def legendre_table(orders):
    colatitude = (jnp.arange(NLAT, dtype=jnp.int32).astype(jnp.float32) + 0.5) * (math.pi / NLAT)
    cosine = jnp.cos(colatitude)[None, :]
    sine_lat = jnp.sin(colatitude)
    order_col = orders.astype(jnp.float32)[:, None]
    log_diag = 0.5 * (lax.lgamma(order_col + 1.5) - lax.lgamma(jnp.float32(1.5)) - lax.lgamma(order_col + 1.0))
    log_diag = log_diag + order_col * jnp.log(sine_lat)[None, :] - 0.5 * math.log(2.0)
    diagonal = jnp.exp(log_diag)
    empty = jnp.zeros_like(diagonal)

    def march_forward(carried, degree):
        previous, current = carried
        deg_float = degree.astype(jnp.float32)
        active = deg_float > order_col
        numerator = jnp.where(active, 4.0 * deg_float * deg_float - 1.0, 1.0)
        bottom = jnp.where(active, deg_float * deg_float - order_col * order_col, 1.0)
        lower_deg = deg_float - 1.0
        retreat = jnp.sqrt(jnp.maximum(lower_deg * lower_deg - order_col * order_col, 0.0) / (4.0 * lower_deg * lower_deg - 1.0))
        grown = jnp.sqrt(numerator / bottom) * (cosine * current - retreat * previous)
        fresh_row = jnp.where(active, grown, jnp.where(deg_float == order_col, diagonal, 0.0))
        return ((current, fresh_row), fresh_row)
    _, legendre_rows = lax.scan(march_forward, (empty, empty), jnp.arange(MMAX, dtype=jnp.int32), unroll=8)
    weights = sine_lat / math.sqrt(NLAT)
    return legendre_rows * weights[None, None, :]

def reference(state, forcing, crm_moisture, cloud_order, wave_table):
    updated = []
    for member in range(ENS):
        member_state = state[member]
        member_force = forcing[member]
        member_moist = crm_moisture[member]

        def per_group(col_group):
            lon_start = col_group * LON_BLOCK
            grid_block = lax.dynamic_slice_in_dim(member_state, lon_start, LON_BLOCK, 3).reshape(F, L, N_LAT, BLOCK_COLS)
            force_block = lax.dynamic_slice_in_dim(member_force, lon_start, LON_BLOCK, 3).reshape(F, L, N_LAT, BLOCK_COLS)
            col_order = lax.dynamic_index_in_dim(cloud_order, col_group, 0, keepdims=False)

            def to_slots(values):
                chosen = jnp.take_along_axis(values, jnp.broadcast_to(col_order[None, None], values.shape), axis=3)
                chosen = chosen.reshape(F, L, N_LAT, TARGETS, PER_TARGET).transpose(0, 1, 3, 2, 4)
                return chosen.reshape(F, L, TARGETS * RUN_COLS)
            vapour_mass_fraction = lax.dynamic_index_in_dim(member_moist, col_group, 3, keepdims=False)
            vapour_mass_fraction = vapour_mass_fraction.astype(jnp.float32).reshape(NCRM, L, TARGETS * RUN_COLS)
            tendencies = cloud_model(to_slots(grid_block), to_slots(force_block), vapour_mass_fraction)
            tendencies = tendencies.reshape(F, L, TARGETS, N_LAT, PER_TARGET).transpose(0, 1, 3, 2, 4)
            tendencies = tendencies.reshape(F, L, N_LAT, BLOCK_COLS)
            inverse = jnp.argsort(col_order, axis=1).astype(jnp.int32)
            restored = jnp.take_along_axis(tendencies, jnp.broadcast_to(inverse[None, None], tendencies.shape), axis=3)
            return restored.reshape(F, L, NLAT, LON_BLOCK)
        pieces = lax.map(per_group, jnp.arange(N_COL, dtype=jnp.int32))
        column_tend = pieces.transpose(1, 2, 3, 0, 4).reshape(F, L, NLAT, NLON)
        updated.append(member_state + column_tend)
    new_state = jnp.stack(updated)
    trig_rows = trig_table(jnp.arange(NLON, dtype=jnp.int32), wave_table)
    fourier = jnp.einsum('eflay,ycs->eflacs', new_state, trig_rows, precision=lax.Precision.HIGHEST)
    weighted = legendre_table(wave_table)
    spectral = jnp.einsum('eflacs,nsa->felscn', fourier, weighted, precision=lax.Precision.HIGHEST)
    return (new_state, spectral)
```

```python
import math

import jax
import jax.numpy as jnp
from jax import lax
from jax.experimental import pallas as pl
from jax.experimental.pallas import tpu as pltpu
from jax.sharding import PartitionSpec as P

NLON = 384
NLAT = 192
MMAX = 128
NSUB = 4
LANES = 128
ROWS = 8

COURANT_SCALE = 0.4
CONDENSE = 0.5


def lane_slice(t):
    return pl.ds(pl.multiple_of(t * LANES, LANES), LANES)


def permute_kernel(x_ref, order_ref, out_ref):
    rows, cols = x_ref.shape
    tiles = cols // LANES

    def one(t, carry):
        order = jnp.broadcast_to(order_ref[:, lane_slice(t)], (ROWS, LANES))
        source = order >> 7
        lane = order & (LANES - 1)
        total = [jnp.zeros((ROWS, LANES), jnp.float32) for _ in range(rows // ROWS)]
        for s in range(tiles):
            hit = source == s
            for r in range(rows // ROWS):
                block = x_ref[r * ROWS : (r + 1) * ROWS, s * LANES : (s + 1) * LANES]
                moved = jnp.take_along_axis(block, lane, axis=1)
                total[r] = jnp.where(hit, moved, total[r])
        for r in range(rows // ROWS):
            out_ref[r * ROWS : (r + 1) * ROWS, lane_slice(t)] = total[r]
        return carry

    lax.fori_loop(0, tiles, one, 0)


def permute(values, order):
    return pl.pallas_call(
        permute_kernel,
        out_shape=jax.ShapeDtypeStruct(values.shape, jnp.float32),
        in_specs=[pl.BlockSpec(memory_space=pltpu.VMEM)] * 2,
        out_specs=pl.BlockSpec(memory_space=pltpu.VMEM),
        name="permute",
    )(values, order)


def cloud_kernel(wind_ref, gap_ref, push_ref, anomaly_ref, rain_ref):
    count, levels, width = anomaly_ref.shape
    scale = CONDENSE / count

    for c0 in range(0, width, LANES):
        c1 = min(c0 + LANES, width)
        for base in range(0, levels, 2 * ROWS):
            top = min(base + 2 * ROWS, levels)
            for r0 in range(base, top, ROWS):
                r1 = min(r0 + ROWS, top)
                courant = COURANT_SCALE * jnp.tanh(wind_ref[r0:r1, c0:c1])
                mixing = 0.2 + 0.5 * jnp.abs(courant)
                ahead = mixing - 0.5 * courant
                back = mixing + 0.5 * courant
                keep = 1.0 - 2.0 * mixing
                push = push_ref[r0:r1, c0:c1]
                start = gap_ref[r0:r1, c0:c1]
                gap = [
                    start
                    + anomaly_ref[n, base:top, c0:c1].astype(jnp.float32)[r0 - base : r1 - base]
                    for n in range(count)
                ]
                rain = [jnp.zeros_like(start) for _ in range(2)]
                for substep in range(NSUB):
                    fresh = []
                    for n in range(count):
                        wet = jnp.maximum(gap[n], 0.0)
                        rain[n % 2] = rain[n % 2] + wet
                        if substep < NSUB - 1:
                            fresh.append(
                                (ahead * gap[(n + 1) % count] + back * gap[n - 1])
                                + (keep * gap[n] + (push - wet))
                            )
                    gap = fresh
                rain_ref[r0:r1, c0:c1] = scale * (rain[0] + rain[1])


def cloud_model(wind, gap, push, anomaly):
    count, levels, width = anomaly.shape
    block = LANES if width % LANES == 0 else width
    flat = pl.BlockSpec((levels, block), lambda i: (0, i))
    return pl.pallas_call(
        cloud_kernel,
        grid=(width // block,),
        out_shape=jax.ShapeDtypeStruct((levels, width), jnp.float32),
        in_specs=[flat, flat, flat, pl.BlockSpec((count, levels, block), lambda i: (0, 0, i))],
        out_specs=flat,
        name="cloud",
    )(wind, gap, push, anomaly)


def legendre_kernel(grow_ref, retreat_ref, order_ref, zero_ref, cosine_ref, diag_ref, fourier_ref, out_ref, *tables):
    slots = order_ref.shape[0]
    halves = len(tables)
    order = order_ref[...]
    grow = grow_ref[...]
    retreat = retreat_ref[...]
    cosine = [cosine_ref[:, h * LANES : (h + 1) * LANES] for h in range(halves)]
    for h in range(halves):
        tables[h][: 2 * slots, :] = jnp.zeros((2 * slots, LANES), jnp.float32)

    def march(n, carry):
        index = zero_ref[...] + n
        grow_n = jnp.take_along_axis(grow, index, axis=1)
        retreat_n = jnp.take_along_axis(retreat, index, axis=1)
        first = order == n
        for h in range(halves):
            previous = tables[h][pl.ds(pl.multiple_of(n * slots, ROWS), slots), :]
            current = tables[h][pl.ds(pl.multiple_of((n + 1) * slots, ROWS), slots), :]
            grown = grow_n * (cosine[h] * current - retreat_n * previous)
            fresh = jnp.where(first, diag_ref[:, h * LANES : (h + 1) * LANES], grown)
            tables[h][pl.ds(pl.multiple_of((n + 2) * slots, ROWS), slots), :] = fresh
        return carry

    lax.fori_loop(0, MMAX, march, 0)

    def contract(s, carry):
        total = None
        for h in range(halves):
            weighted = tables[h][pl.ds(2 * slots + s, MMAX, stride=slots), :]
            term = lax.dot_general(
                fourier_ref[s, :, h * LANES : (h + 1) * LANES],
                weighted,
                (((1,), (1,)), ((), ())),
                precision=lax.Precision.HIGHEST,
                preferred_element_type=jnp.float32,
            )
            total = term if total is None else total + term
        out_ref[s] = total
        return carry

    lax.fori_loop(0, slots, contract, 0)


def legendre(orders, fourier):
    slots, terms, lats = fourier.shape
    wide = -(-lats // LANES) * LANES
    colatitude = (jnp.arange(lats, dtype=jnp.int32).astype(jnp.float32) + 0.5) * (math.pi / lats)
    sine_lat = jnp.sin(colatitude)
    order_col = orders.astype(jnp.float32)[:, None]
    log_diag = 0.5 * (
        lax.lgamma(order_col + 1.5) - lax.lgamma(jnp.float32(1.5)) - lax.lgamma(order_col + 1.0)
    )
    log_diag = log_diag + order_col * jnp.log(sine_lat)[None, :] - 0.5 * math.log(2.0)
    diagonal = jnp.exp(log_diag) * (sine_lat / math.sqrt(lats))[None, :]
    degree = jnp.arange(MMAX, dtype=jnp.int32).astype(jnp.float32)[None, :]
    active = degree > order_col
    numerator = jnp.where(active, 4.0 * degree * degree - 1.0, 0.0)
    bottom = jnp.where(active, degree * degree - order_col * order_col, 1.0)
    lower = degree - 1.0
    retreat = jnp.sqrt(
        jnp.maximum(lower * lower - order_col * order_col, 0.0) / (4.0 * lower * lower - 1.0)
    )
    grow = jnp.sqrt(numerator / bottom)
    pad = ((0, 0), (0, wide - lats))
    return pl.pallas_call(
        legendre_kernel,
        out_shape=jax.ShapeDtypeStruct((slots, terms, MMAX), jnp.float32),
        in_specs=[pl.BlockSpec(memory_space=pltpu.VMEM)] * 7,
        out_specs=pl.BlockSpec(memory_space=pltpu.VMEM),
        scratch_shapes=[pltpu.VMEM(((MMAX + 2) * slots, LANES), jnp.float32)] * (wide // LANES),
        name="legendre",
    )(
        grow,
        retreat,
        jnp.broadcast_to(orders[:, None], (slots, LANES)),
        jnp.zeros((slots, LANES), jnp.int32),
        jnp.pad(jnp.cos(colatitude)[None, :], pad),
        jnp.pad(diagonal, pad),
        jnp.pad(fourier, ((0, 0),) + pad),
    )


def trig_table(longitudes, wave_numbers):
    phase = (longitudes[:, None] * wave_numbers[None, :] % NLON).astype(jnp.float32) * (
        2.0 * math.pi / NLON
    )
    return jnp.stack((jnp.cos(phase), jnp.sin(phase)), axis=1) / math.sqrt(NLON)


def inverse_order(order):
    cols = order.shape[0]
    tiles = cols // LANES
    slots = jnp.arange(cols, dtype=jnp.int32)
    high = (order[None, :] // LANES) == jnp.arange(tiles, dtype=jnp.int32)[:, None]
    low = (order[:, None] % LANES) == jnp.arange(LANES, dtype=jnp.int32)[None, :]
    digits = jnp.stack((slots // LANES, slots % LANES)).astype(jnp.bfloat16)
    left = jnp.where(high[None], digits[:, None, :], jnp.bfloat16(0)).reshape(2 * tiles, cols)
    found = jnp.dot(left, low.astype(jnp.bfloat16), preferred_element_type=jnp.float32)
    found = found.reshape(2, cols).astype(jnp.int32)
    return found[0] * LANES + found[1]


def shards(state, forcing, crm_moisture, cloud_order, wave_table):
    members, _, levels, band_rows, lon_block = state.shape
    sections = lax.axis_size("sec")
    lat_bands = lax.axis_size("lat")
    block_cols = band_rows * lon_block
    targets = sections * lat_bands
    per_target = block_cols // targets
    run_cols = lat_bands * per_target
    padded = -(-levels // ROWS) * ROWS
    field = lax.axis_index("sec")
    slot_list = cloud_order[0, 0]
    own, force = state[0, 0], forcing[0, 0]

    mate = lax.ppermute(jnp.where(field == 2, force, own), "sec", [(2, 3), (3, 2)])
    part = jnp.where(
        field == 3, (force - mate) / NSUB, jnp.where(field == 2, mate - own, own)
    )
    flat = jnp.pad(part.reshape(levels, block_cols), ((0, padded - levels), (0, 0)))
    in_slots = permute(flat, slot_list[None, :])[:levels]
    outgoing = in_slots.reshape(levels, targets, per_target).transpose(1, 0, 2)
    arrived = lax.all_to_all(outgoing, ("sec", "lat"), split_axis=0, concat_axis=0, tiled=True)
    arrived = arrived.reshape(sections, lat_bands, levels, per_target).transpose(0, 2, 1, 3)
    arrived = arrived.reshape(sections, levels, run_cols)
    rain = cloud_model(arrived[0], arrived[2], arrived[3], crm_moisture[0, :, :, 0, 0, :])
    homeward = rain.reshape(levels, lat_bands, per_target).transpose(1, 0, 2)
    homeward = jnp.broadcast_to(homeward[None], (sections, lat_bands, levels, per_target))
    homeward = homeward.reshape(targets, levels, per_target)
    returned = lax.all_to_all(homeward, ("sec", "lat"), split_axis=0, concat_axis=0, tiled=True)
    returned = returned.transpose(1, 0, 2).reshape(levels, block_cols)
    returned = jnp.pad(returned, ((0, padded - levels), (0, 0)))
    rainfall = permute(returned, inverse_order(slot_list)[None, :])[:levels]
    rainfall = rainfall.reshape(levels, band_rows, lon_block)
    share = jnp.where(
        field < 2, own * (-1.0 / NSUB), jnp.where(field == 2, jnp.float32(1), jnp.float32(-1))
    )
    fresh = own + (share * rainfall + force)

    regrouped = lax.all_to_all(fresh, "col", split_axis=0, concat_axis=2, tiled=True)
    trig_rows = trig_table(jnp.arange(NLON, dtype=jnp.int32), wave_table)
    spectra = jnp.einsum("lay,ycs->slca", regrouped, trig_rows, precision=lax.Precision.HIGHEST)
    owner_count = MMAX // lat_bands
    owned_waves = lax.dynamic_slice_in_dim(
        wave_table, lax.axis_index("lat") * owner_count, owner_count
    )
    gathered = lax.all_to_all(spectra, "lat", split_axis=0, concat_axis=3, tiled=True)
    own_levels = gathered.shape[1]
    coeffs = legendre(owned_waves, gathered.reshape(owner_count, own_levels * 2, NLAT))
    coeffs = coeffs.reshape(owner_count, own_levels, 2, MMAX).transpose(1, 0, 2, 3)
    return (fresh[None, None], coeffs[None, None])


def solution(mesh):
    placed = (
        P(None, "sec", None, "lat", "col"),
        P(None, "sec", None, "lat", "col"),
        P(None, None, None, ("sec", "lat"), "col", None),
        P("col", "lat", None),
        P(),
    )
    return jax.shard_map(
        shards,
        mesh=mesh,
        in_specs=placed,
        out_specs=(P(None, "sec", None, "lat", "col"), P("sec", None, "col", "lat", None, None)),
        check_vma=False,
    )
```

```python
import math

import jax
import jax.numpy as jnp
from jax import lax
from jax.experimental import pallas as pl
from jax.experimental.pallas import tpu as pltpu
from jax.sharding import PartitionSpec as P

NLON = 384
NLAT = 192
MMAX = 128
NSUB = 4
LANES = 128
ROWS = 8

COURANT_SCALE = 0.4
CONDENSE = 0.5


def permute_kernel(x_ref, order_ref, out_ref, parts):
    rows, cols = x_ref.shape
    tiles = cols // LANES
    width = 2 * LANES if tiles % 2 == 0 else LANES
    batch = tiles // 3 if tiles % 3 == 0 else tiles

    for s in range(tiles):
        block = x_ref[:, s * LANES : (s + 1) * LANES]
        coarse = block.astype(jnp.bfloat16)
        parts[s * rows : (s + 1) * rows, :LANES] = coarse
        parts[s * rows : (s + 1) * rows, LANES:] = (block - coarse.astype(jnp.float32)).astype(
            jnp.bfloat16
        )
    wanted = lax.broadcasted_iota(jnp.int32, (2 * LANES, width), 0) & (LANES - 1)

    def one(t, carry):
        at = pl.ds(pl.multiple_of(t * width, width), width)
        order = order_ref[:, at]
        source = jnp.broadcast_to(order >> 7, (ROWS, width))
        chosen = jnp.where(wanted == (order & (LANES - 1)), 1.0, 0.0).astype(jnp.bfloat16)
        total = [jnp.zeros((ROWS, width), jnp.float32) for _ in range(rows // ROWS)]
        for first in range(0, tiles, batch):
            moved = jnp.dot(
                parts[first * rows : (first + batch) * rows, :],
                chosen,
                preferred_element_type=jnp.float32,
            )
            for s in range(batch):
                hit = source == first + s
                for r in range(rows // ROWS):
                    begin = s * rows + r * ROWS
                    total[r] = jnp.where(hit, moved[begin : begin + ROWS], total[r])
        for r in range(rows // ROWS):
            out_ref[r * ROWS : (r + 1) * ROWS, at] = total[r]
        return carry

    lax.fori_loop(0, cols // width, one, 0)


def permute(values, order):
    return pl.pallas_call(
        permute_kernel,
        out_shape=jax.ShapeDtypeStruct(values.shape, jnp.float32),
        in_specs=[pl.BlockSpec(memory_space=pltpu.VMEM)] * 2,
        out_specs=pl.BlockSpec(memory_space=pltpu.VMEM),
        scratch_shapes=[
            pltpu.VMEM((values.shape[0] * values.shape[1] // LANES, 2 * LANES), jnp.bfloat16)
        ],
        name="permute",
    )(values, order)


def cloud_kernel(wind_ref, gap_ref, push_ref, anomaly_ref, rain_ref):
    count, levels, width = anomaly_ref.shape
    scale = CONDENSE / count

    for c0 in range(0, width, LANES):
        c1 = min(c0 + LANES, width)
        for base in range(0, levels, 2 * ROWS):
            top = min(base + 2 * ROWS, levels)
            for r0 in range(base, top, ROWS):
                r1 = min(r0 + ROWS, top)
                courant = COURANT_SCALE * jnp.tanh(wind_ref[r0:r1, c0:c1])
                mixing = 0.2 + 0.5 * jnp.abs(courant)
                ahead = mixing - 0.5 * courant
                back = mixing + 0.5 * courant
                keep = 1.0 - 2.0 * mixing
                push = push_ref[r0:r1, c0:c1]
                start = gap_ref[r0:r1, c0:c1]
                gap = [
                    start
                    + anomaly_ref[n, base:top, c0:c1].astype(jnp.float32)[r0 - base : r1 - base]
                    for n in range(count)
                ]
                rain = [jnp.zeros_like(start) for _ in range(2)]
                for substep in range(NSUB):
                    fresh = []
                    for n in range(count):
                        wet = jnp.maximum(gap[n], 0.0)
                        rain[n % 2] = rain[n % 2] + wet
                        if substep < NSUB - 1:
                            fresh.append(
                                (ahead * gap[(n + 1) % count] + back * gap[n - 1])
                                + (keep * gap[n] + (push - wet))
                            )
                    gap = fresh
                rain_ref[r0:r1, c0:c1] = scale * (rain[0] + rain[1])


def cloud_model(wind, gap, push, anomaly):
    count, levels, width = anomaly.shape
    block = LANES if width % LANES == 0 else width
    flat = pl.BlockSpec((levels, block), lambda i: (0, i))
    return pl.pallas_call(
        cloud_kernel,
        grid=(width // block,),
        out_shape=jax.ShapeDtypeStruct((levels, width), jnp.float32),
        in_specs=[flat, flat, flat, pl.BlockSpec((count, levels, block), lambda i: (0, 0, i))],
        out_specs=flat,
        name="cloud",
    )(wind, gap, push, anomaly)


def march_kernel(grow_ref, retreat_ref, order_ref, zero_ref, cosine_ref, diag_ref, *tables):
    slots = order_ref.shape[0]
    halves = len(tables)
    order = order_ref[...]
    grow = grow_ref[...]
    retreat = retreat_ref[...]
    cosine = [cosine_ref[:, h * LANES : (h + 1) * LANES] for h in range(halves)]
    for h in range(halves):
        tables[h][: 2 * slots, :] = jnp.zeros((2 * slots, LANES), jnp.float32)

    def march(n, carry):
        index = zero_ref[...] + n
        grow_n = jnp.take_along_axis(grow, index, axis=1)
        retreat_n = jnp.take_along_axis(retreat, index, axis=1)
        first = order == n
        for h in range(halves):
            previous = tables[h][pl.ds(pl.multiple_of(n * slots, ROWS), slots), :]
            current = tables[h][pl.ds(pl.multiple_of((n + 1) * slots, ROWS), slots), :]
            grown = grow_n * (cosine[h] * current - retreat_n * previous)
            fresh = jnp.where(first, diag_ref[:, h * LANES : (h + 1) * LANES], grown)
            tables[h][pl.ds(pl.multiple_of((n + 2) * slots, ROWS), slots), :] = fresh
        return carry

    lax.fori_loop(0, MMAX, march, 0)


def contract_kernel(fourier_ref, *refs):
    *tables, out_ref = refs
    slots, terms, _ = fourier_ref.shape
    group = 4 if slots % 4 == 0 else 1

    def split(values):
        coarse = values.astype(jnp.bfloat16)
        return coarse, (values - coarse.astype(jnp.float32)).astype(jnp.bfloat16)

    def product(left, right):
        return lax.dot_general(
            left, right, (((1,), (1,)), ((), ())), preferred_element_type=jnp.float32
        )

    def contract(g, carry):
        for j in range(group):
            s = g * group + j
            weighted = jnp.concatenate(
                [table[pl.ds(2 * slots + s, MMAX, stride=slots), :] for table in tables], axis=1
            )
            coarse, fine = split(weighted)
            head, rest = split(fourier_ref[s])
            main = product(jnp.concatenate([head, rest], axis=0), coarse)
            out_ref[s] = main[:terms] + main[terms:] + product(head, fine)
        return carry

    lax.fori_loop(0, slots // group, contract, 0)


def legendre_tables(orders, lats):
    slots = orders.shape[0]
    wide = -(-lats // LANES) * LANES
    colatitude = (jnp.arange(lats, dtype=jnp.int32).astype(jnp.float32) + 0.5) * (math.pi / lats)
    sine_lat = jnp.sin(colatitude)
    order_col = orders.astype(jnp.float32)[:, None]
    log_diag = 0.5 * (
        lax.lgamma(order_col + 1.5) - lax.lgamma(jnp.float32(1.5)) - lax.lgamma(order_col + 1.0)
    )
    log_diag = log_diag + order_col * jnp.log(sine_lat)[None, :] - 0.5 * math.log(2.0)
    diagonal = jnp.exp(log_diag) * (sine_lat / math.sqrt(lats))[None, :]
    degree = jnp.arange(MMAX, dtype=jnp.int32).astype(jnp.float32)[None, :]
    active = degree > order_col
    numerator = jnp.where(active, 4.0 * degree * degree - 1.0, 0.0)
    bottom = jnp.where(active, degree * degree - order_col * order_col, 1.0)
    lower = degree - 1.0
    retreat = jnp.sqrt(
        jnp.maximum(lower * lower - order_col * order_col, 0.0) / (4.0 * lower * lower - 1.0)
    )
    grow = jnp.sqrt(numerator / bottom)
    pad = ((0, 0), (0, wide - lats))
    table = jax.ShapeDtypeStruct(((MMAX + 2) * slots, LANES), jnp.float32)
    return pl.pallas_call(
        march_kernel,
        out_shape=[table] * (wide // LANES),
        in_specs=[pl.BlockSpec(memory_space=pltpu.VMEM)] * 6,
        out_specs=[pl.BlockSpec(memory_space=pltpu.VMEM)] * (wide // LANES),
        cost_estimate=pl.CostEstimate(
            flops=6 * MMAX * slots * wide, bytes_accessed=16 * MMAX * slots * wide, transcendentals=0
        ),
        name="march",
    )(
        grow,
        retreat,
        jnp.broadcast_to(orders[:, None], (slots, LANES)),
        jnp.zeros((slots, LANES), jnp.int32),
        jnp.pad(jnp.cos(colatitude)[None, :], pad),
        jnp.pad(diagonal, pad),
    )


def contract_tables(fourier, tables):
    slots, terms, lats = fourier.shape
    wide = len(tables) * LANES
    padded = -(-terms // 16) * 16
    fourier = jnp.pad(fourier, ((0, 0), (0, padded - terms), (0, wide - lats)))
    found = pl.pallas_call(
        contract_kernel,
        out_shape=jax.ShapeDtypeStruct((slots, padded, MMAX), jnp.float32),
        in_specs=[pl.BlockSpec(memory_space=pltpu.VMEM)] * (1 + len(tables)),
        out_specs=pl.BlockSpec(memory_space=pltpu.VMEM),
        name="contract",
    )(fourier, *tables)
    return found[:, :terms]


def trig_table(longitudes, wave_numbers):
    phase = (longitudes[:, None] * wave_numbers[None, :] % NLON).astype(jnp.float32) * (
        2.0 * math.pi / NLON
    )
    return jnp.stack((jnp.cos(phase), jnp.sin(phase)), axis=1) / math.sqrt(NLON)


def inverse_order(order):
    cols = order.shape[0]
    tiles = cols // LANES
    slots = jnp.arange(cols, dtype=jnp.int32)
    high = (order[None, :] // LANES) == jnp.arange(tiles, dtype=jnp.int32)[:, None]
    low = (order[:, None] % LANES) == jnp.arange(LANES, dtype=jnp.int32)[None, :]
    digits = jnp.stack((slots // LANES, slots % LANES)).astype(jnp.bfloat16)
    left = jnp.where(high[None], digits[:, None, :], jnp.bfloat16(0)).reshape(2 * tiles, cols)
    found = jnp.dot(left, low.astype(jnp.bfloat16), preferred_element_type=jnp.float32)
    found = found.reshape(2, cols).astype(jnp.int32)
    return found[0] * LANES + found[1]


def shards(state, forcing, crm_moisture, cloud_order, wave_table):
    members, _, levels, band_rows, lon_block = state.shape
    sections = lax.axis_size("sec")
    lat_bands = lax.axis_size("lat")
    block_cols = band_rows * lon_block
    targets = sections * lat_bands
    per_target = block_cols // targets
    run_cols = lat_bands * per_target
    padded = -(-levels // ROWS) * ROWS
    field = lax.axis_index("sec")
    slot_list = cloud_order[0, 0]
    own, force = state[0, 0], forcing[0, 0]

    mate = lax.ppermute(jnp.where(field == 2, force, own), "sec", [(2, 3), (3, 2)])
    part = jnp.where(
        field == 3, (force - mate) / NSUB, jnp.where(field == 2, mate - own, own)
    )
    flat = jnp.pad(part.reshape(levels, block_cols), ((0, padded - levels), (0, 0)))
    in_slots = permute(flat, slot_list[None, :])[:levels]
    outgoing = in_slots.reshape(levels, targets, per_target).transpose(1, 0, 2)
    crm_moisture, outgoing = lax.optimization_barrier((crm_moisture, outgoing))
    arrived = lax.all_to_all(outgoing, ("sec", "lat"), split_axis=0, concat_axis=0, tiled=True)
    arrived = arrived.reshape(sections, lat_bands, levels, per_target).transpose(0, 2, 1, 3)
    arrived = arrived.reshape(sections, levels, run_cols)
    rain = cloud_model(arrived[0], arrived[2], arrived[3], crm_moisture[0, :, :, 0, 0, :])
    homeward = rain.reshape(levels, lat_bands, per_target).transpose(1, 0, 2)
    homeward = jnp.broadcast_to(homeward[None], (sections, lat_bands, levels, per_target))
    homeward = homeward.reshape(targets, levels, per_target)
    returned = lax.all_to_all(homeward, ("sec", "lat"), split_axis=0, concat_axis=0, tiled=True)
    returned = returned.transpose(1, 0, 2).reshape(levels, block_cols)
    returned = jnp.pad(returned, ((0, padded - levels), (0, 0)))
    rainfall = permute(returned, inverse_order(slot_list)[None, :])[:levels]
    rainfall = rainfall.reshape(levels, band_rows, lon_block)
    share = jnp.where(
        field < 2, own * (-1.0 / NSUB), jnp.where(field == 2, jnp.float32(1), jnp.float32(-1))
    )
    fresh = own + (share * rainfall + force)

    regrouped = lax.all_to_all(fresh, "col", split_axis=0, concat_axis=2, tiled=True)
    trig_rows = trig_table(jnp.arange(NLON, dtype=jnp.int32), wave_table)
    spectra = jnp.einsum("lay,ycs->slca", regrouped, trig_rows, precision=lax.Precision.HIGHEST)
    owner_count = MMAX // lat_bands
    wave_table, _ = lax.optimization_barrier((wave_table, rainfall))
    owned_waves = lax.dynamic_slice_in_dim(
        wave_table, lax.axis_index("lat") * owner_count, owner_count
    )
    gathered = lax.all_to_all(spectra, "lat", split_axis=0, concat_axis=3, tiled=True)
    own_levels = gathered.shape[1]
    coeffs = contract_tables(
        gathered.reshape(owner_count, own_levels * 2, NLAT), legendre_tables(owned_waves, NLAT)
    )
    coeffs = coeffs.reshape(owner_count, own_levels, 2, MMAX).transpose(1, 0, 2, 3)
    return (fresh[None, None], coeffs[None, None])


def solution(mesh):
    placed = (
        P(None, "sec", None, "lat", "col"),
        P(None, "sec", None, "lat", "col"),
        P(None, None, None, ("sec", "lat"), "col", None),
        P("col", "lat", None),
        P(),
    )
    return jax.shard_map(
        shards,
        mesh=mesh,
        in_specs=placed,
        out_specs=(P(None, "sec", None, "lat", "col"), P("sec", None, "col", "lat", None, None)),
        check_vma=False,
    )
```

```python
import math

import jax
import jax.numpy as jnp
from jax import lax
from jax.experimental import pallas as pl
from jax.experimental.pallas import tpu as pltpu
from jax.sharding import PartitionSpec as P

NLON = 384
NLAT = 192
MMAX = 128
NSUB = 4
LANES = 128
ROWS = 8

COURANT_SCALE = 0.4
CONDENSE = 0.5


def permute_kernel(x_ref, order_ref, out_ref, parts, held):
    levels = x_ref.shape[-2]
    rows = held.shape[0]
    cols = order_ref.shape[1]
    tiles = cols // LANES
    gathered = held.shape[1] // LANES
    multiplied = tiles - gathered
    halves = 2 if tiles % 2 == 0 else 1
    width = halves * LANES
    fill = jnp.zeros((rows - levels, LANES), jnp.float32)
    groups = range(rows // ROWS)

    for s in range(tiles):
        if x_ref.ndim == 2:
            block = x_ref[:, s * LANES : (s + 1) * LANES]
        else:
            per = x_ref.shape[2] // LANES
            block = x_ref[s // per, :, s % per * LANES : (s % per + 1) * LANES]
        if rows > levels:
            block = jnp.concatenate([block, fill], axis=0)
        if s < multiplied:
            coarse = block.astype(jnp.bfloat16)
            parts[s * rows : (s + 1) * rows, :LANES] = coarse
            parts[s * rows : (s + 1) * rows, LANES:] = (
                block - coarse.astype(jnp.float32)
            ).astype(jnp.bfloat16)
        else:
            held[:, (s - multiplied) * LANES : (s - multiplied + 1) * LANES] = block
    wanted = lax.broadcasted_iota(jnp.int32, (2 * LANES, width), 0) & (LANES - 1)

    def one(t, carry):
        order = order_ref[:, pl.ds(pl.multiple_of(t * width, width), width)]
        lane = order & (LANES - 1)
        chosen = jnp.where(wanted == lane, 1.0, 0.0).astype(jnp.bfloat16)
        moved = jnp.dot(parts[...], chosen, preferred_element_type=jnp.float32)
        for h in range(halves):
            mine = slice(h * LANES, (h + 1) * LANES)
            source = jnp.broadcast_to(order[:, mine] >> 7, (ROWS, LANES))
            lanes = jnp.broadcast_to(lane[:, mine], (ROWS, LANES))
            total = [jnp.zeros((ROWS, LANES), jnp.float32) for _ in groups]
            for s in range(gathered):
                hit = source == multiplied + s
                for r in groups:
                    block = held[r * ROWS : (r + 1) * ROWS, s * LANES : (s + 1) * LANES]
                    total[r] = jnp.where(hit, jnp.take_along_axis(block, lanes, axis=1), total[r])
            for s in range(multiplied):
                hit = source == s
                for r in groups:
                    begin = s * rows + r * ROWS
                    total[r] = jnp.where(hit, moved[begin : begin + ROWS, mine], total[r])
            tile = t * halves + h
            for r in groups:
                end = min((r + 1) * ROWS, levels)
                value = total[r][: end - r * ROWS]
                if out_ref.ndim == 2:
                    at = pl.ds(pl.multiple_of(tile * LANES, LANES), LANES)
                    out_ref[r * ROWS : end, at] = value
                else:
                    per = out_ref.shape[2] // LANES
                    at = pl.ds(pl.multiple_of(tile % per * LANES, LANES), LANES)
                    out_ref[tile // per, r * ROWS : end, at] = value
        return carry

    lax.fori_loop(0, tiles // halves, one, 0)


def permute(values, order, shape):
    levels, tiles = values.shape[-2], order.shape[1] // LANES
    rows = -(-levels // ROWS) * ROWS
    gathered = tiles * 3 // 8
    return pl.pallas_call(
        permute_kernel,
        out_shape=jax.ShapeDtypeStruct(shape, jnp.float32),
        in_specs=[pl.BlockSpec(memory_space=pltpu.VMEM)] * 2,
        out_specs=pl.BlockSpec(memory_space=pltpu.VMEM),
        scratch_shapes=[
            pltpu.VMEM(((tiles - gathered) * rows, 2 * LANES), jnp.bfloat16),
            pltpu.VMEM((rows, gathered * LANES), jnp.float32),
        ],
        name="permute",
    )(values, order)


def cloud_kernel(wind_ref, gap_ref, push_ref, anomaly_ref, rain_ref):
    count, levels, width = anomaly_ref.shape
    scale = CONDENSE / count

    for c0 in range(0, width, LANES):
        c1 = min(c0 + LANES, width)
        for base in range(0, levels, 2 * ROWS):
            top = min(base + 2 * ROWS, levels)
            for r0 in range(base, top, ROWS):
                r1 = min(r0 + ROWS, top)
                courant = COURANT_SCALE * jnp.tanh(wind_ref[r0:r1, c0:c1])
                mixing = 0.2 + 0.5 * jnp.abs(courant)
                ahead = mixing - 0.5 * courant
                back = mixing + 0.5 * courant
                keep = 1.0 - 2.0 * mixing
                push = push_ref[r0:r1, c0:c1]
                start = gap_ref[r0:r1, c0:c1]
                gap = [
                    start
                    + anomaly_ref[n, base:top, c0:c1].astype(jnp.float32)[r0 - base : r1 - base]
                    for n in range(count)
                ]
                rain = [jnp.zeros_like(start) for _ in range(2)]
                for substep in range(NSUB):
                    fresh = []
                    for n in range(count):
                        wet = jnp.maximum(gap[n], 0.0)
                        rain[n % 2] = rain[n % 2] + wet
                        if substep < NSUB - 1:
                            fresh.append(
                                (ahead * gap[(n + 1) % count] + back * gap[n - 1])
                                + (keep * gap[n] + (push - wet))
                            )
                    gap = fresh
                found = scale * (rain[0] + rain[1])
                for copy in range(rain_ref.shape[0]):
                    rain_ref[copy, r0:r1, c0:c1] = found


def cloud_model(arrived, anomaly, sections):
    count, levels, _ = anomaly.shape
    blocks, _, span = arrived.shape
    bands = blocks // sections
    block = LANES if span % LANES == 0 else span
    steps = span // block
    if block < LANES:
        anomaly = anomaly.reshape(count, levels, bands, span).transpose(2, 0, 1, 3)
        moist = pl.BlockSpec((None, count, levels, span), lambda i: (i, 0, 0, 0))
    else:
        moist = pl.BlockSpec((count, levels, block), lambda i: (0, 0, i))

    def of(field):
        return pl.BlockSpec(
            (None, levels, block), lambda i: (field * bands + i // steps, 0, i % steps)
        )

    found = pl.pallas_call(
        cloud_kernel,
        grid=(bands * steps,),
        out_shape=jax.ShapeDtypeStruct((sections, bands, levels, span), jnp.float32),
        in_specs=[of(0), of(2), of(3), moist],
        out_specs=pl.BlockSpec(
            (sections, None, levels, block), lambda i: (0, i // steps, 0, i % steps)
        ),
        name="cloud",
    )(arrived, arrived, arrived, anomaly)
    return found.reshape(arrived.shape)


def march_kernel(grow_ref, retreat_ref, order_ref, zero_ref, cosine_ref, diag_ref, *tables):
    slots = order_ref.shape[0]
    halves = len(tables)
    order = order_ref[...]
    grow = grow_ref[...]
    retreat = retreat_ref[...]
    cosine = [cosine_ref[:, h * LANES : (h + 1) * LANES] for h in range(halves)]
    for h in range(halves):
        tables[h][: 2 * slots, :] = jnp.zeros((2 * slots, LANES), jnp.float32)
    group = 8

    def march(g, carry):
        begin = g * group
        held = [
            [
                tables[h][pl.ds(pl.multiple_of((begin + j) * slots, ROWS), slots), :]
                for j in range(2)
            ]
            for h in range(halves)
        ]
        for j in range(group):
            n = begin + j
            index = zero_ref[...] + n
            grow_n = jnp.take_along_axis(grow, index, axis=1)
            retreat_n = jnp.take_along_axis(retreat, index, axis=1)
            first = order == n
            for h in range(halves):
                previous, current = held[h]
                grown = grow_n * (cosine[h] * current - retreat_n * previous)
                fresh = jnp.where(first, diag_ref[:, h * LANES : (h + 1) * LANES], grown)
                tables[h][pl.ds(pl.multiple_of((n + 2) * slots, ROWS), slots), :] = fresh
                held[h] = [current, fresh]
        return carry

    lax.fori_loop(0, MMAX // group, march, 0)


def contract_kernel(fourier_ref, *refs):
    *tables, out_ref = refs
    slots, terms, _ = fourier_ref.shape
    group = 4 if slots % 4 == 0 else 1

    def split(values):
        coarse = values.astype(jnp.bfloat16)
        return coarse, (values - coarse.astype(jnp.float32)).astype(jnp.bfloat16)

    def product(left, right):
        return lax.dot_general(
            left, right, (((1,), (1,)), ((), ())), preferred_element_type=jnp.float32
        )

    def contract(g, carry):
        for j in range(group):
            s = g * group + j
            weighted = jnp.concatenate(
                [table[pl.ds(2 * slots + s, MMAX, stride=slots), :] for table in tables], axis=1
            )
            coarse, fine = split(weighted)
            head, rest = split(fourier_ref[s])
            main = product(jnp.concatenate([head, rest], axis=0), coarse)
            out_ref[s] = main[:terms] + main[terms:] + product(head, fine)
        return carry

    lax.fori_loop(0, slots // group, contract, 0)


def legendre_tables(orders, lats):
    slots = orders.shape[0]
    wide = -(-lats // LANES) * LANES
    colatitude = (jnp.arange(lats, dtype=jnp.int32).astype(jnp.float32) + 0.5) * (math.pi / lats)
    sine_lat = jnp.sin(colatitude)
    order_col = orders.astype(jnp.float32)[:, None]
    log_diag = 0.5 * (
        lax.lgamma(order_col + 1.5) - lax.lgamma(jnp.float32(1.5)) - lax.lgamma(order_col + 1.0)
    )
    log_diag = log_diag + order_col * jnp.log(sine_lat)[None, :] - 0.5 * math.log(2.0)
    diagonal = jnp.exp(log_diag) * (sine_lat / math.sqrt(lats))[None, :]
    degree = jnp.arange(MMAX, dtype=jnp.int32).astype(jnp.float32)[None, :]
    active = degree > order_col
    numerator = jnp.where(active, 4.0 * degree * degree - 1.0, 0.0)
    bottom = jnp.where(active, degree * degree - order_col * order_col, 1.0)
    lower = degree - 1.0
    retreat = jnp.sqrt(
        jnp.maximum(lower * lower - order_col * order_col, 0.0) / (4.0 * lower * lower - 1.0)
    )
    grow = jnp.sqrt(numerator / bottom)
    pad = ((0, 0), (0, wide - lats))
    table = jax.ShapeDtypeStruct(((MMAX + 2) * slots, LANES), jnp.float32)
    return pl.pallas_call(
        march_kernel,
        out_shape=[table] * (wide // LANES),
        in_specs=[pl.BlockSpec(memory_space=pltpu.VMEM)] * 6,
        out_specs=[pl.BlockSpec(memory_space=pltpu.VMEM)] * (wide // LANES),
        cost_estimate=pl.CostEstimate(
            flops=6 * MMAX * slots * wide, bytes_accessed=16 * MMAX * slots * wide, transcendentals=0
        ),
        name="march",
    )(
        grow,
        retreat,
        jnp.broadcast_to(orders[:, None], (slots, LANES)),
        jnp.zeros((slots, LANES), jnp.int32),
        jnp.pad(jnp.cos(colatitude)[None, :], pad),
        jnp.pad(diagonal, pad),
    )


def contract_tables(fourier, tables):
    slots, terms, lats = fourier.shape
    wide = len(tables) * LANES
    padded = -(-terms // 16) * 16
    fourier = jnp.pad(fourier, ((0, 0), (0, padded - terms), (0, wide - lats)))
    found = pl.pallas_call(
        contract_kernel,
        out_shape=jax.ShapeDtypeStruct((slots, padded, MMAX), jnp.float32),
        in_specs=[pl.BlockSpec(memory_space=pltpu.VMEM)] * (1 + len(tables)),
        out_specs=pl.BlockSpec(memory_space=pltpu.VMEM),
        name="contract",
    )(fourier, *tables)
    return found[:, :terms]


def trig_table(longitudes, wave_numbers):
    phase = (longitudes[:, None] * wave_numbers[None, :] % NLON).astype(jnp.float32) * (
        2.0 * math.pi / NLON
    )
    return jnp.stack((jnp.cos(phase), jnp.sin(phase)), axis=1) / math.sqrt(NLON)


def inverse_order(order):
    cols = order.shape[0]
    tiles = cols // LANES
    slots = jnp.arange(cols, dtype=jnp.int32)
    high = (order[None, :] // LANES) == jnp.arange(tiles, dtype=jnp.int32)[:, None]
    low = (order[:, None] % LANES) == jnp.arange(LANES, dtype=jnp.int32)[None, :]
    digits = jnp.stack((slots // LANES, slots % LANES)).astype(jnp.bfloat16)
    left = jnp.where(high[None], digits[:, None, :], jnp.bfloat16(0)).reshape(2 * tiles, cols)
    found = jnp.dot(left, low.astype(jnp.bfloat16), preferred_element_type=jnp.float32)
    found = found.reshape(2, cols).astype(jnp.int32)
    return found[0] * LANES + found[1]


def shards(state, forcing, crm_moisture, cloud_order, wave_table):
    members, _, levels, band_rows, lon_block = state.shape
    sections = lax.axis_size("sec")
    lat_bands = lax.axis_size("lat")
    block_cols = band_rows * lon_block
    targets = sections * lat_bands
    per_target = block_cols // targets
    field = lax.axis_index("sec")
    slot_list = cloud_order[0, 0]
    own, force = state[0, 0], forcing[0, 0]

    mate = lax.ppermute(jnp.where(field == 2, force, own), "sec", [(2, 3), (3, 2)])
    part = jnp.where(
        field == 3, (force - mate) / NSUB, jnp.where(field == 2, mate - own, own)
    )
    flat = part.reshape(levels, block_cols)
    cut = (targets, levels, per_target)
    tiled = per_target % LANES == 0
    if tiled:
        outgoing = permute(flat, slot_list[None, :], cut)
    else:
        in_slots = permute(flat, slot_list[None, :], flat.shape)
        outgoing = in_slots.reshape(levels, targets, per_target).transpose(1, 0, 2)
    crm_moisture, outgoing = lax.optimization_barrier((crm_moisture, outgoing))
    arrived = lax.all_to_all(outgoing, ("sec", "lat"), split_axis=0, concat_axis=0, tiled=True)
    homeward = cloud_model(arrived, crm_moisture[0, :, :, 0, 0, :], sections)
    returned = lax.all_to_all(homeward, ("sec", "lat"), split_axis=0, concat_axis=0, tiled=True)
    if not tiled:
        returned = returned.transpose(1, 0, 2).reshape(levels, block_cols)
    rainfall = permute(returned, inverse_order(slot_list)[None, :], flat.shape)
    rainfall = rainfall.reshape(levels, band_rows, lon_block)
    share = jnp.where(
        field < 2, own * (-1.0 / NSUB), jnp.where(field == 2, jnp.float32(1), jnp.float32(-1))
    )
    fresh = own + (share * rainfall + force)

    regrouped = lax.all_to_all(fresh, "col", split_axis=0, concat_axis=2, tiled=True)
    trig_rows = trig_table(jnp.arange(NLON, dtype=jnp.int32), wave_table)
    spectra = jnp.einsum("lay,ycs->slca", regrouped, trig_rows, precision=lax.Precision.HIGHEST)
    owner_count = MMAX // lat_bands
    wave_table, _ = lax.optimization_barrier((wave_table, rainfall))
    owned_waves = lax.dynamic_slice_in_dim(
        wave_table, lax.axis_index("lat") * owner_count, owner_count
    )
    gathered = lax.all_to_all(spectra, "lat", split_axis=0, concat_axis=3, tiled=True)
    own_levels = gathered.shape[1]
    coeffs = contract_tables(
        gathered.reshape(owner_count, own_levels * 2, NLAT), legendre_tables(owned_waves, NLAT)
    )
    coeffs = coeffs.reshape(owner_count, own_levels, 2, MMAX).transpose(1, 0, 2, 3)
    return (fresh[None, None], coeffs[None, None])


def solution(mesh):
    placed = (
        P(None, "sec", None, "lat", "col"),
        P(None, "sec", None, "lat", "col"),
        P(None, None, None, ("sec", "lat"), "col", None),
        P("col", "lat", None),
        P(),
    )
    return jax.shard_map(
        shards,
        mesh=mesh,
        in_specs=placed,
        out_specs=(P(None, "sec", None, "lat", "col"), P("sec", None, "col", "lat", None, None)),
        check_vma=False,
    )
```

```python
import math

import jax
import jax.numpy as jnp
from jax import lax
from jax.experimental import pallas as pl
from jax.experimental.pallas import tpu as pltpu
from jax.sharding import PartitionSpec as P

NLON = 384
NLAT = 192
MMAX = 128
NSUB = 4
LANES = 128
ROWS = 8

COURANT_SCALE = 0.4
CONDENSE = 0.5


def permute_kernel(x_ref, order_ref, out_ref, parts, held):
    levels = x_ref.shape[-2]
    rows = held.shape[0]
    cols = order_ref.shape[1]
    tiles = cols // LANES
    gathered = held.shape[1] // LANES
    multiplied = tiles - gathered
    halves = 2 if tiles % 2 == 0 else 1
    width = halves * LANES
    fill = jnp.zeros((rows - levels, LANES), jnp.float32)
    groups = range(rows // ROWS)

    for s in range(tiles):
        if x_ref.ndim == 2:
            block = x_ref[:, s * LANES : (s + 1) * LANES]
        else:
            per = x_ref.shape[2] // LANES
            block = x_ref[s // per, :, s % per * LANES : (s % per + 1) * LANES]
        if rows > levels:
            block = jnp.concatenate([block, fill], axis=0)
        if s < multiplied:
            coarse = block.astype(jnp.bfloat16)
            parts[s * rows : (s + 1) * rows, :LANES] = coarse
            parts[s * rows : (s + 1) * rows, LANES:] = (
                block - coarse.astype(jnp.float32)
            ).astype(jnp.bfloat16)
        else:
            held[:, (s - multiplied) * LANES : (s - multiplied + 1) * LANES] = block
    wanted = lax.broadcasted_iota(jnp.int32, (2 * LANES, width), 0) & (LANES - 1)

    def one(t, carry):
        order = order_ref[:, pl.ds(pl.multiple_of(t * width, width), width)]
        lane = order & (LANES - 1)
        chosen = jnp.where(wanted == lane, 1.0, 0.0).astype(jnp.bfloat16)
        moved = jnp.dot(parts[...], chosen, preferred_element_type=jnp.float32)
        for h in range(halves):
            mine = slice(h * LANES, (h + 1) * LANES)
            source = jnp.broadcast_to(order[:, mine] >> 7, (ROWS, LANES))
            lanes = jnp.broadcast_to(lane[:, mine], (ROWS, LANES))
            total = [jnp.zeros((ROWS, LANES), jnp.float32) for _ in groups]
            for s in range(gathered):
                hit = source == multiplied + s
                for r in groups:
                    block = held[r * ROWS : (r + 1) * ROWS, s * LANES : (s + 1) * LANES]
                    total[r] = jnp.where(hit, jnp.take_along_axis(block, lanes, axis=1), total[r])
            for s in range(multiplied):
                hit = source == s
                for r in groups:
                    begin = s * rows + r * ROWS
                    total[r] = jnp.where(hit, moved[begin : begin + ROWS, mine], total[r])
            tile = t * halves + h
            for r in groups:
                end = min((r + 1) * ROWS, levels)
                value = total[r][: end - r * ROWS]
                if out_ref.ndim == 2:
                    at = pl.ds(pl.multiple_of(tile * LANES, LANES), LANES)
                    out_ref[r * ROWS : end, at] = value
                else:
                    per = out_ref.shape[2] // LANES
                    at = pl.ds(pl.multiple_of(tile % per * LANES, LANES), LANES)
                    out_ref[tile // per, r * ROWS : end, at] = value
        return carry

    lax.fori_loop(0, tiles // halves, one, 0)


def permute(values, order, shape):
    levels, tiles = values.shape[-2], order.shape[1] // LANES
    rows = -(-levels // ROWS) * ROWS
    gathered = tiles * 3 // 8
    return pl.pallas_call(
        permute_kernel,
        out_shape=jax.ShapeDtypeStruct(shape, jnp.float32),
        in_specs=[pl.BlockSpec(memory_space=pltpu.VMEM)] * 2,
        out_specs=pl.BlockSpec(memory_space=pltpu.VMEM),
        scratch_shapes=[
            pltpu.VMEM(((tiles - gathered) * rows, 2 * LANES), jnp.bfloat16),
            pltpu.VMEM((rows, gathered * LANES), jnp.float32),
        ],
        name="permute",
    )(values, order)


def cloud_kernel(wind_ref, gap_ref, push_ref, anomaly_ref, rain_ref):
    count, levels, width = anomaly_ref.shape
    scale = CONDENSE / count

    for c0 in range(0, width, LANES):
        c1 = min(c0 + LANES, width)
        for base in range(0, levels, 2 * ROWS):
            top = min(base + 2 * ROWS, levels)
            for r0 in range(base, top, ROWS):
                r1 = min(r0 + ROWS, top)
                courant = COURANT_SCALE * jnp.tanh(wind_ref[r0:r1, c0:c1])
                mixing = 0.2 + 0.5 * jnp.abs(courant)
                ahead = mixing - 0.5 * courant
                back = mixing + 0.5 * courant
                keep = 1.0 - 2.0 * mixing
                push = push_ref[r0:r1, c0:c1]
                start = gap_ref[r0:r1, c0:c1]
                gap = [
                    start
                    + anomaly_ref[n, base:top, c0:c1].astype(jnp.float32)[r0 - base : r1 - base]
                    for n in range(count)
                ]
                rain = [jnp.zeros_like(start) for _ in range(2)]
                for substep in range(NSUB):
                    fresh = []
                    for n in range(count):
                        wet = jnp.maximum(gap[n], 0.0)
                        rain[n % 2] = rain[n % 2] + wet
                        if substep < NSUB - 1:
                            fresh.append(
                                (ahead * gap[(n + 1) % count] + back * gap[n - 1])
                                + (keep * gap[n] + (push - wet))
                            )
                    gap = fresh
                found = scale * (rain[0] + rain[1])
                for copy in range(rain_ref.shape[0]):
                    rain_ref[copy, r0:r1, c0:c1] = found


def cloud_model(arrived, anomaly, sections):
    count, levels, _ = anomaly.shape
    blocks, _, span = arrived.shape
    bands = blocks // sections
    block = LANES if span % LANES == 0 else span
    steps = span // block
    if block < LANES:
        anomaly = anomaly.reshape(count, levels, bands, span).transpose(2, 0, 1, 3)
        moist = pl.BlockSpec((None, count, levels, span), lambda i: (i, 0, 0, 0))
    else:
        moist = pl.BlockSpec((count, levels, block), lambda i: (0, 0, i))

    def of(field):
        return pl.BlockSpec(
            (None, levels, block), lambda i: (field * bands + i // steps, 0, i % steps)
        )

    found = pl.pallas_call(
        cloud_kernel,
        grid=(bands * steps,),
        out_shape=jax.ShapeDtypeStruct((sections, bands, levels, span), jnp.float32),
        in_specs=[of(0), of(2), of(3), moist],
        out_specs=pl.BlockSpec(
            (sections, None, levels, block), lambda i: (0, i // steps, 0, i % steps)
        ),
        name="cloud",
    )(arrived, arrived, arrived, anomaly)
    return found.reshape(arrived.shape)


def halve(values):
    coarse = values.astype(jnp.bfloat16)
    return coarse, (values - coarse.astype(jnp.float32)).astype(jnp.bfloat16)


def march_kernel(
    grow_ref, retreat_ref, order_ref, zero_ref, cosine_ref, diag_ref, coarse_ref, fine_ref, *tables
):
    slots = order_ref.shape[0]
    halves = len(tables)
    order = order_ref[...]
    grow = grow_ref[...]
    retreat = retreat_ref[...]
    cosine = [cosine_ref[:, h * LANES : (h + 1) * LANES] for h in range(halves)]
    for h in range(halves):
        tables[h][: 2 * slots, :] = jnp.zeros((2 * slots, LANES), jnp.float32)
    group = 8

    def march(g, carry):
        begin = g * group
        held = [
            [
                tables[h][pl.ds(pl.multiple_of((begin + j) * slots, ROWS), slots), :]
                for j in range(2)
            ]
            for h in range(halves)
        ]
        for j in range(group):
            n = begin + j
            index = zero_ref[...] + n
            grow_n = jnp.take_along_axis(grow, index, axis=1)
            retreat_n = jnp.take_along_axis(retreat, index, axis=1)
            first = order == n
            for h in range(halves):
                previous, current = held[h]
                grown = grow_n * (cosine[h] * current - retreat_n * previous)
                fresh = jnp.where(first, diag_ref[:, h * LANES : (h + 1) * LANES], grown)
                tables[h][pl.ds(pl.multiple_of((n + 2) * slots, ROWS), slots), :] = fresh
                held[h] = [current, fresh]
        return carry

    lax.fori_loop(0, MMAX // group, march, 0)

    def sort(g, carry):
        for j in range(4):
            s = g * 4 + j
            for h in range(halves):
                rows = tables[h][pl.ds(2 * slots + s, MMAX, stride=slots), :]
                mine = slice(h * LANES, (h + 1) * LANES)
                coarse_ref[s, :, mine], fine_ref[s, :, mine] = halve(rows)
        return carry

    lax.fori_loop(0, slots // 4, sort, 0)


def contract_kernel(fourier_ref, coarse_ref, fine_ref, out_ref):
    levels, slots, _, _ = out_ref.shape
    bands = fourier_ref.shape[0]
    terms = 2 * levels
    rows = -(-terms // 16) * 16

    def product(left, right):
        return lax.dot_general(
            left, right, (((1,), (1,)), ((), ())), preferred_element_type=jnp.float32
        )

    def contract(g, carry):
        for j in range(4):
            s = g * 4 + j
            found = [fourier_ref[b, pl.ds(s, terms, stride=slots), :] for b in range(bands)]
            found = jnp.concatenate(found, axis=1)
            if rows > terms:
                fill = jnp.zeros((rows - terms, found.shape[1]), jnp.float32)
                found = jnp.concatenate([found, fill], axis=0)
            head, rest = halve(found)
            main = product(jnp.concatenate([head, rest], axis=0), coarse_ref[s])
            total = main[:rows] + main[rows:] + product(head, fine_ref[s])
            for l in range(levels):
                out_ref[l, s] = total[2 * l : 2 * l + 2]
        return carry

    lax.fori_loop(0, slots // 4, contract, 0)


def dft_kernel(x_ref, trig_ref, out_ref):
    blocks, levels, lats, _ = x_ref.shape
    parts, _, _, slots, lanes = out_ref.shape
    count = trig_ref.shape[1]
    waves = [jnp.concatenate(halve(trig_ref[j]), axis=0) for j in range(blocks)]

    def product(left, right):
        return lax.dot_general(
            left, right, (((1,), (1,)), ((), ())), preferred_element_type=jnp.float32
        )

    for first in range(0, levels, 2):
        last = min(first + 2, levels)
        total = None
        for j in range(blocks):
            grid = []
            for l in range(first, last):
                grid.append(x_ref[j, l])
                if lanes > lats:
                    grid.append(jnp.zeros((lanes - lats, x_ref.shape[3]), jnp.float32))
            coarse, fine = halve(jnp.concatenate(grid, axis=0))
            main = product(waves[j], coarse)
            term = main[:count] + main[count:] + product(waves[j][:count], fine)
            total = term if total is None else total + term
        for l in range(first, last):
            mine = total[:, (l - first) * lanes : (l - first + 1) * lanes]
            for p in range(parts):
                for c in range(2):
                    begin = (p * 2 + c) * slots
                    out_ref[p, l, c] = mine[begin : begin + slots]


def dft(regrouped, wave_table, blocks, parts):
    _, lats, lons = regrouped.shape
    levels = regrouped.shape[0] // blocks
    slots = wave_table.shape[0] // parts
    pad = -lats % ROWS
    lanes = -(-lats // LANES) * LANES
    grid = jnp.pad(regrouped, ((0, 0), (0, pad), (0, 0)))
    trig = trig_table(jnp.arange(NLON, dtype=jnp.int32), wave_table)
    trig = trig.reshape(blocks, lons, 2, parts, slots).transpose(0, 3, 2, 4, 1)
    return pl.pallas_call(
        dft_kernel,
        out_shape=jax.ShapeDtypeStruct((parts, levels, 2, slots, lanes), jnp.float32),
        in_specs=[pl.BlockSpec(memory_space=pltpu.VMEM)] * 2,
        out_specs=pl.BlockSpec(memory_space=pltpu.VMEM),
        name="dft",
    )(
        grid.reshape(blocks, levels, lats + pad, lons),
        trig.reshape(blocks, 2 * parts * slots, lons),
    )


def legendre_tables(orders, lats, bands):
    slots = orders.shape[0]
    wide = bands * (-(-(lats // bands) // LANES) * LANES)
    colatitude = (jnp.arange(lats, dtype=jnp.int32).astype(jnp.float32) + 0.5) * (math.pi / lats)
    sine_lat = jnp.sin(colatitude)
    order_col = orders.astype(jnp.float32)[:, None]
    log_diag = 0.5 * (
        lax.lgamma(order_col + 1.5) - lax.lgamma(jnp.float32(1.5)) - lax.lgamma(order_col + 1.0)
    )
    log_diag = log_diag + order_col * jnp.log(sine_lat)[None, :] - 0.5 * math.log(2.0)
    diagonal = jnp.exp(log_diag) * (sine_lat / math.sqrt(lats))[None, :]
    degree = jnp.arange(MMAX, dtype=jnp.int32).astype(jnp.float32)[None, :]
    active = degree > order_col
    numerator = jnp.where(active, 4.0 * degree * degree - 1.0, 0.0)
    bottom = jnp.where(active, degree * degree - order_col * order_col, 1.0)
    lower = degree - 1.0
    retreat = jnp.sqrt(
        jnp.maximum(lower * lower - order_col * order_col, 0.0) / (4.0 * lower * lower - 1.0)
    )
    grow = jnp.sqrt(numerator / bottom)

    def spread(values):
        cut = values.reshape(values.shape[0], bands, lats // bands)
        cut = jnp.pad(cut, ((0, 0), (0, 0), (0, wide // bands - lats // bands)))
        return cut.reshape(values.shape[0], wide)

    table = jax.ShapeDtypeStruct((slots, MMAX, wide), jnp.bfloat16)
    return pl.pallas_call(
        march_kernel,
        out_shape=[table] * 2,
        in_specs=[pl.BlockSpec(memory_space=pltpu.VMEM)] * 6,
        out_specs=[pl.BlockSpec(memory_space=pltpu.VMEM)] * 2,
        scratch_shapes=[pltpu.VMEM(((MMAX + 2) * slots, LANES), jnp.float32)] * (wide // LANES),
        cost_estimate=pl.CostEstimate(
            flops=6 * MMAX * slots * wide, bytes_accessed=16 * MMAX * slots * wide, transcendentals=0
        ),
        name="march",
    )(
        grow,
        retreat,
        jnp.broadcast_to(orders[:, None], (slots, LANES)),
        jnp.zeros((slots, LANES), jnp.int32),
        spread(jnp.cos(colatitude)[None, :]),
        spread(diagonal),
    )


def contract_tables(fourier, tables):
    bands, levels, _, slots, lanes = fourier.shape
    return pl.pallas_call(
        contract_kernel,
        out_shape=jax.ShapeDtypeStruct((levels, slots, 2, MMAX), jnp.float32),
        in_specs=[pl.BlockSpec(memory_space=pltpu.VMEM)] * 3,
        out_specs=pl.BlockSpec(memory_space=pltpu.VMEM),
        name="contract",
    )(fourier.reshape(bands, levels * 2 * slots, lanes), *tables)


def trig_table(longitudes, wave_numbers):
    phase = (longitudes[:, None] * wave_numbers[None, :] % NLON).astype(jnp.float32) * (
        2.0 * math.pi / NLON
    )
    return jnp.stack((jnp.cos(phase), jnp.sin(phase)), axis=1) / math.sqrt(NLON)


def inverse_order(order):
    cols = order.shape[0]
    tiles = cols // LANES
    slots = jnp.arange(cols, dtype=jnp.int32)
    high = (order[None, :] // LANES) == jnp.arange(tiles, dtype=jnp.int32)[:, None]
    low = (order[:, None] % LANES) == jnp.arange(LANES, dtype=jnp.int32)[None, :]
    digits = jnp.stack((slots // LANES, slots % LANES)).astype(jnp.bfloat16)
    left = jnp.where(high[None], digits[:, None, :], jnp.bfloat16(0)).reshape(2 * tiles, cols)
    found = jnp.dot(left, low.astype(jnp.bfloat16), preferred_element_type=jnp.float32)
    found = found.reshape(2, cols).astype(jnp.int32)
    return found[0] * LANES + found[1]


def shards(state, forcing, crm_moisture, cloud_order, wave_table):
    members, _, levels, band_rows, lon_block = state.shape
    sections = lax.axis_size("sec")
    lat_bands = lax.axis_size("lat")
    block_cols = band_rows * lon_block
    targets = sections * lat_bands
    per_target = block_cols // targets
    field = lax.axis_index("sec")
    slot_list = cloud_order[0, 0]
    own, force = state[0, 0], forcing[0, 0]

    mate = lax.ppermute(jnp.where(field == 2, force, own), "sec", [(2, 3), (3, 2)])
    part = jnp.where(
        field == 3, (force - mate) / NSUB, jnp.where(field == 2, mate - own, own)
    )
    flat = part.reshape(levels, block_cols)
    cut = (targets, levels, per_target)
    tiled = per_target % LANES == 0
    if tiled:
        outgoing = permute(flat, slot_list[None, :], cut)
    else:
        in_slots = permute(flat, slot_list[None, :], flat.shape)
        outgoing = in_slots.reshape(levels, targets, per_target).transpose(1, 0, 2)
    crm_moisture, outgoing = lax.optimization_barrier((crm_moisture, outgoing))
    arrived = lax.all_to_all(outgoing, ("sec", "lat"), split_axis=0, concat_axis=0, tiled=True)
    homeward = cloud_model(arrived, crm_moisture[0, :, :, 0, 0, :], sections)
    returned = lax.all_to_all(homeward, ("sec", "lat"), split_axis=0, concat_axis=0, tiled=True)
    if not tiled:
        returned = returned.transpose(1, 0, 2).reshape(levels, block_cols)
    rainfall = permute(returned, inverse_order(slot_list)[None, :], flat.shape)
    rainfall = rainfall.reshape(levels, band_rows, lon_block)
    share = jnp.where(
        field < 2, own * (-1.0 / NSUB), jnp.where(field == 2, jnp.float32(1), jnp.float32(-1))
    )
    fresh = own + (share * rainfall + force)

    regrouped = lax.all_to_all(fresh, "col", split_axis=0, concat_axis=0, tiled=True)
    spectra = dft(regrouped, wave_table, lax.axis_size("col"), lat_bands)
    owner_count = MMAX // lat_bands
    wave_table, _ = lax.optimization_barrier((wave_table, rainfall))
    owned_waves = lax.dynamic_slice_in_dim(
        wave_table, lax.axis_index("lat") * owner_count, owner_count
    )
    gathered = lax.all_to_all(spectra, "lat", split_axis=0, concat_axis=0, tiled=True)
    coeffs = contract_tables(gathered, legendre_tables(owned_waves, NLAT, lat_bands))
    return (fresh[None, None], coeffs[None, None])


def solution(mesh):
    placed = (
        P(None, "sec", None, "lat", "col"),
        P(None, "sec", None, "lat", "col"),
        P(None, None, None, ("sec", "lat"), "col", None),
        P("col", "lat", None),
        P(),
    )
    return jax.shard_map(
        shards,
        mesh=mesh,
        in_specs=placed,
        out_specs=(P(None, "sec", None, "lat", "col"), P("sec", None, "col", "lat", None, None)),
        check_vma=False,
    )
```

```python
import math

import jax
import jax.numpy as jnp
from jax import lax
from jax.experimental import pallas as pl
from jax.experimental.pallas import tpu as pltpu
from jax.sharding import PartitionSpec as P

NLON = 384
NLAT = 192
MMAX = 128
NSUB = 4
LANES = 128
ROWS = 8

COURANT_SCALE = 0.4
CONDENSE = 0.5


def permute_kernel(x_ref, order_ref, out_ref, parts, held):
    levels = x_ref.shape[-2]
    rows = held.shape[0]
    cols = order_ref.shape[1]
    tiles = cols // LANES
    gathered = held.shape[1] // LANES
    multiplied = tiles - gathered
    halves = 2 if tiles % 2 == 0 else 1
    width = halves * LANES
    fill = jnp.zeros((rows - levels, LANES), jnp.float32)
    groups = range(rows // ROWS)

    for s in range(tiles):
        if x_ref.ndim == 2:
            block = x_ref[:, s * LANES : (s + 1) * LANES]
        else:
            per = x_ref.shape[2] // LANES
            block = x_ref[s // per, :, s % per * LANES : (s % per + 1) * LANES]
        if rows > levels:
            block = jnp.concatenate([block, fill], axis=0)
        if s < multiplied:
            coarse = block.astype(jnp.bfloat16)
            parts[s * rows : (s + 1) * rows, :LANES] = coarse
            parts[s * rows : (s + 1) * rows, LANES:] = (
                block - coarse.astype(jnp.float32)
            ).astype(jnp.bfloat16)
        else:
            held[:, (s - multiplied) * LANES : (s - multiplied + 1) * LANES] = block
    wanted = lax.broadcasted_iota(jnp.int32, (2 * LANES, width), 0) & (LANES - 1)

    def one(t, carry):
        order = order_ref[:, pl.ds(pl.multiple_of(t * width, width), width)]
        lane = order & (LANES - 1)
        chosen = jnp.where(wanted == lane, 1.0, 0.0).astype(jnp.bfloat16)
        moved = jnp.dot(parts[...], chosen, preferred_element_type=jnp.float32)
        for h in range(halves):
            mine = slice(h * LANES, (h + 1) * LANES)
            source = jnp.broadcast_to(order[:, mine] >> 7, (ROWS, LANES))
            lanes = jnp.broadcast_to(lane[:, mine], (ROWS, LANES))
            total = [jnp.zeros((ROWS, LANES), jnp.float32) for _ in groups]
            for s in range(gathered):
                hit = source == multiplied + s
                for r in groups:
                    block = held[r * ROWS : (r + 1) * ROWS, s * LANES : (s + 1) * LANES]
                    total[r] = jnp.where(hit, jnp.take_along_axis(block, lanes, axis=1), total[r])
            for s in range(multiplied):
                hit = source == s
                for r in groups:
                    begin = s * rows + r * ROWS
                    total[r] = jnp.where(hit, moved[begin : begin + ROWS, mine], total[r])
            tile = t * halves + h
            for r in groups:
                end = min((r + 1) * ROWS, levels)
                value = total[r][: end - r * ROWS]
                if out_ref.ndim == 2:
                    at = pl.ds(pl.multiple_of(tile * LANES, LANES), LANES)
                    out_ref[r * ROWS : end, at] = value
                else:
                    per = out_ref.shape[2] // LANES
                    at = pl.ds(pl.multiple_of(tile % per * LANES, LANES), LANES)
                    out_ref[tile // per, r * ROWS : end, at] = value
        return carry

    lax.fori_loop(0, tiles // halves, one, 0)


def permute(values, order, shape):
    levels, tiles = values.shape[-2], order.shape[1] // LANES
    rows = -(-levels // ROWS) * ROWS
    gathered = tiles * 3 // 8
    return pl.pallas_call(
        permute_kernel,
        out_shape=jax.ShapeDtypeStruct(shape, jnp.float32),
        in_specs=[pl.BlockSpec(memory_space=pltpu.VMEM)] * 2,
        out_specs=pl.BlockSpec(memory_space=pltpu.VMEM),
        scratch_shapes=[
            pltpu.VMEM(((tiles - gathered) * rows, 2 * LANES), jnp.bfloat16),
            pltpu.VMEM((rows, gathered * LANES), jnp.float32),
        ],
        name="permute",
    )(values, order)


def cloud_kernel(wind_ref, gap_ref, push_ref, anomaly_ref, rain_ref):
    count, levels, width = anomaly_ref.shape
    scale = CONDENSE / count

    for c0 in range(0, width, LANES):
        c1 = min(c0 + LANES, width)
        for base in range(0, levels, 2 * ROWS):
            top = min(base + 2 * ROWS, levels)
            for r0 in range(base, top, ROWS):
                r1 = min(r0 + ROWS, top)
                courant = COURANT_SCALE * jnp.tanh(wind_ref[r0:r1, c0:c1])
                mixing = 0.2 + 0.5 * jnp.abs(courant)
                ahead = mixing - 0.5 * courant
                back = mixing + 0.5 * courant
                keep = 1.0 - 2.0 * mixing
                push = push_ref[r0:r1, c0:c1]
                start = gap_ref[r0:r1, c0:c1]
                gap = [
                    start
                    + anomaly_ref[n, base:top, c0:c1].astype(jnp.float32)[r0 - base : r1 - base]
                    for n in range(count)
                ]
                rain = [jnp.zeros_like(start) for _ in range(2)]
                for substep in range(NSUB):
                    fresh = []
                    for n in range(count):
                        wet = jnp.maximum(gap[n], 0.0)
                        rain[n % 2] = rain[n % 2] + wet
                        if substep < NSUB - 1:
                            fresh.append(
                                (ahead * gap[(n + 1) % count] + back * gap[n - 1])
                                + (keep * gap[n] + (push - wet))
                            )
                    gap = fresh
                found = scale * (rain[0] + rain[1])
                for copy in range(rain_ref.shape[0]):
                    rain_ref[copy, r0:r1, c0:c1] = found


def cloud_model(arrived, anomaly, sections):
    count, levels, _ = anomaly.shape
    blocks, _, span = arrived.shape
    bands = blocks // sections
    block = LANES if span % LANES == 0 else span
    steps = span // block
    if block < LANES:
        anomaly = anomaly.reshape(count, levels, bands, span).transpose(2, 0, 1, 3)
        moist = pl.BlockSpec((None, count, levels, span), lambda i: (i, 0, 0, 0))
    else:
        moist = pl.BlockSpec((count, levels, block), lambda i: (0, 0, i))

    def of(field):
        return pl.BlockSpec(
            (None, levels, block), lambda i: (field * bands + i // steps, 0, i % steps)
        )

    found = pl.pallas_call(
        cloud_kernel,
        grid=(bands * steps,),
        out_shape=jax.ShapeDtypeStruct((sections, bands, levels, span), jnp.float32),
        in_specs=[of(0), of(2), of(3), moist],
        out_specs=pl.BlockSpec(
            (sections, None, levels, block), lambda i: (0, i // steps, 0, i % steps)
        ),
        name="cloud",
    )(arrived, arrived, arrived, anomaly)
    return found.reshape(arrived.shape)


def halve(values):
    coarse = values.astype(jnp.bfloat16)
    return coarse, (values - coarse.astype(jnp.float32)).astype(jnp.bfloat16)


def march_kernel(
    grow_ref, retreat_ref, order_ref, zero_ref, cosine_ref, diag_ref, coarse_ref, fine_ref, *tables
):
    slots = order_ref.shape[0]
    halves = len(tables)
    order = order_ref[...]
    grow = grow_ref[...]
    retreat = retreat_ref[...]
    cosine = [cosine_ref[:, h * LANES : (h + 1) * LANES] for h in range(halves)]
    for h in range(halves):
        tables[h][: 2 * slots, :] = jnp.zeros((2 * slots, LANES), jnp.float32)
    group = 8

    def march(g, carry):
        begin = g * group
        held = [
            [
                tables[h][pl.ds(pl.multiple_of((begin + j) * slots, ROWS), slots), :]
                for j in range(2)
            ]
            for h in range(halves)
        ]
        for j in range(group):
            n = begin + j
            index = zero_ref[...] + n
            grow_n = jnp.take_along_axis(grow, index, axis=1)
            retreat_n = jnp.take_along_axis(retreat, index, axis=1)
            first = order == n
            for h in range(halves):
                previous, current = held[h]
                grown = grow_n * (cosine[h] * current - retreat_n * previous)
                fresh = jnp.where(first, diag_ref[:, h * LANES : (h + 1) * LANES], grown)
                tables[h][pl.ds(pl.multiple_of((n + 2) * slots, ROWS), slots), :] = fresh
                held[h] = [current, fresh]
        return carry

    lax.fori_loop(0, MMAX // group, march, 0)

    def sort(g, carry):
        for j in range(4):
            s = g * 4 + j
            for h in range(halves):
                rows = tables[h][pl.ds(2 * slots + s, MMAX, stride=slots), :]
                mine = slice(h * LANES, (h + 1) * LANES)
                coarse_ref[s, :, mine], fine_ref[s, :, mine] = halve(rows)
        return carry

    lax.fori_loop(0, slots // 4, sort, 0)


def contract_kernel(fourier_ref, coarse_ref, fine_ref, out_ref):
    levels, slots, _, _ = out_ref.shape
    bands = fourier_ref.shape[0]
    terms = 2 * levels
    rows = -(-terms // 16) * 16

    def product(left, right):
        return lax.dot_general(
            left, right, (((1,), (1,)), ((), ())), preferred_element_type=jnp.float32
        )

    def contract(g, carry):
        for j in range(4):
            s = g * 4 + j
            found = [fourier_ref[b, pl.ds(s, terms, stride=slots), :] for b in range(bands)]
            found = jnp.concatenate(found, axis=1)
            if rows > terms:
                fill = jnp.zeros((rows - terms, found.shape[1]), jnp.float32)
                found = jnp.concatenate([found, fill], axis=0)
            head, rest = halve(found)
            main = product(jnp.concatenate([head, rest], axis=0), coarse_ref[s])
            total = main[:rows] + main[rows:] + product(head, fine_ref[s])
            for l in range(levels):
                out_ref[l, s] = total[2 * l : 2 * l + 2]
        return carry

    lax.fori_loop(0, slots // 4, contract, 0)


def dft_kernel(x_ref, trig_ref, out_ref):
    blocks, levels, lats, _ = x_ref.shape
    parts, _, _, slots, lanes = out_ref.shape
    count = trig_ref.shape[1]
    waves = [jnp.concatenate(halve(trig_ref[j]), axis=0) for j in range(blocks)]

    def product(left, right):
        return lax.dot_general(
            left, right, (((1,), (1,)), ((), ())), preferred_element_type=jnp.float32
        )

    for first in range(0, levels, 2):
        last = min(first + 2, levels)
        total = None
        for j in range(blocks):
            grid = []
            for l in range(first, last):
                grid.append(x_ref[j, l])
                if lanes > lats:
                    grid.append(jnp.zeros((lanes - lats, x_ref.shape[3]), jnp.float32))
            coarse, fine = halve(jnp.concatenate(grid, axis=0))
            main = product(waves[j], coarse)
            term = main[:count] + main[count:] + product(waves[j][:count], fine)
            total = term if total is None else total + term
        for l in range(first, last):
            mine = total[:, (l - first) * lanes : (l - first + 1) * lanes]
            for p in range(parts):
                for c in range(2):
                    begin = (p * 2 + c) * slots
                    out_ref[p, l, c] = mine[begin : begin + slots]


def dft(regrouped, wave_table, blocks, parts):
    _, lats, lons = regrouped.shape
    levels = regrouped.shape[0] // blocks
    slots = wave_table.shape[0] // parts
    pad = -lats % ROWS
    lanes = -(-lats // LANES) * LANES
    grid = jnp.pad(regrouped, ((0, 0), (0, pad), (0, 0)))
    trig = trig_table(jnp.arange(NLON, dtype=jnp.int32), wave_table)
    trig = trig.reshape(blocks, lons, 2, parts, slots).transpose(0, 3, 2, 4, 1)
    return pl.pallas_call(
        dft_kernel,
        out_shape=jax.ShapeDtypeStruct((parts, levels, 2, slots, lanes), jnp.float32),
        in_specs=[pl.BlockSpec(memory_space=pltpu.VMEM)] * 2,
        out_specs=pl.BlockSpec(memory_space=pltpu.VMEM),
        name="dft",
    )(
        grid.reshape(blocks, levels, lats + pad, lons),
        trig.reshape(blocks, 2 * parts * slots, lons),
    )


def legendre_tables(orders, lats, bands):
    slots = orders.shape[0]
    wide = bands * (-(-(lats // bands) // LANES) * LANES)
    colatitude = (jnp.arange(lats, dtype=jnp.int32).astype(jnp.float32) + 0.5) * (math.pi / lats)
    sine_lat = jnp.sin(colatitude)
    order_col = orders.astype(jnp.float32)[:, None]
    log_diag = 0.5 * (
        lax.lgamma(order_col + 1.5) - lax.lgamma(jnp.float32(1.5)) - lax.lgamma(order_col + 1.0)
    )
    log_diag = log_diag + order_col * jnp.log(sine_lat)[None, :] - 0.5 * math.log(2.0)
    diagonal = jnp.exp(log_diag) * (sine_lat / math.sqrt(lats))[None, :]
    degree = jnp.arange(MMAX, dtype=jnp.int32).astype(jnp.float32)[None, :]
    active = degree > order_col
    numerator = jnp.where(active, 4.0 * degree * degree - 1.0, 0.0)
    bottom = jnp.where(active, degree * degree - order_col * order_col, 1.0)
    lower = degree - 1.0
    retreat = jnp.sqrt(
        jnp.maximum(lower * lower - order_col * order_col, 0.0) / (4.0 * lower * lower - 1.0)
    )
    grow = jnp.sqrt(numerator / bottom)

    def spread(values):
        cut = values.reshape(values.shape[0], bands, lats // bands)
        cut = jnp.pad(cut, ((0, 0), (0, 0), (0, wide // bands - lats // bands)))
        return cut.reshape(values.shape[0], wide)

    table = jax.ShapeDtypeStruct((slots, MMAX, wide), jnp.bfloat16)
    return pl.pallas_call(
        march_kernel,
        out_shape=[table] * 2,
        in_specs=[pl.BlockSpec(memory_space=pltpu.VMEM)] * 6,
        out_specs=[pl.BlockSpec(memory_space=pltpu.VMEM)] * 2,
        scratch_shapes=[pltpu.VMEM(((MMAX + 2) * slots, LANES), jnp.float32)] * (wide // LANES),
        cost_estimate=pl.CostEstimate(
            flops=6 * MMAX * slots * wide, bytes_accessed=16 * MMAX * slots * wide, transcendentals=0
        ),
        name="march",
    )(
        grow,
        retreat,
        jnp.broadcast_to(orders[:, None], (slots, LANES)),
        jnp.zeros((slots, LANES), jnp.int32),
        spread(jnp.cos(colatitude)[None, :]),
        spread(diagonal),
    )


def contract_tables(fourier, tables):
    bands, levels, _, slots, lanes = fourier.shape
    return pl.pallas_call(
        contract_kernel,
        out_shape=jax.ShapeDtypeStruct((levels, slots, 2, MMAX), jnp.float32),
        in_specs=[pl.BlockSpec(memory_space=pltpu.VMEM)] * 3,
        out_specs=pl.BlockSpec(memory_space=pltpu.VMEM),
        name="contract",
    )(fourier.reshape(bands, levels * 2 * slots, lanes), *tables)


def trig_table(longitudes, wave_numbers):
    phase = (longitudes[:, None] * wave_numbers[None, :] % NLON).astype(jnp.float32) * (
        2.0 * math.pi / NLON
    )
    return jnp.stack((jnp.cos(phase), jnp.sin(phase)), axis=1) / math.sqrt(NLON)


def inverse_order(order):
    cols = order.shape[0]
    tiles = cols // LANES
    slots = jnp.arange(cols, dtype=jnp.int32)
    high = (order[None, :] // LANES) == jnp.arange(tiles, dtype=jnp.int32)[:, None]
    low = (order[:, None] % LANES) == jnp.arange(LANES, dtype=jnp.int32)[None, :]
    digits = jnp.stack((slots // LANES, slots % LANES)).astype(jnp.bfloat16)
    left = jnp.where(high[None], digits[:, None, :], jnp.bfloat16(0)).reshape(2 * tiles, cols)
    found = jnp.dot(left, low.astype(jnp.bfloat16), preferred_element_type=jnp.float32)
    found = found.reshape(2, cols).astype(jnp.int32)
    return found[0] * LANES + found[1]


def shards(state, forcing, crm_moisture, cloud_order, wave_table):
    members, _, levels, band_rows, lon_block = state.shape
    sections = lax.axis_size("sec")
    lat_bands = lax.axis_size("lat")
    block_cols = band_rows * lon_block
    targets = sections * lat_bands
    per_target = block_cols // targets
    field = lax.axis_index("sec")
    slot_list = cloud_order[0, 0]
    own, force = state[0, 0], forcing[0, 0]

    mate = lax.ppermute(jnp.where(field == 2, force, own), "sec", [(2, 3), (3, 2)])
    part = jnp.where(
        field == 3, (force - mate) / NSUB, jnp.where(field == 2, mate - own, own)
    )
    flat = part.reshape(levels, block_cols)
    cut = (targets, levels, per_target)
    tiled = per_target % LANES == 0
    if tiled:
        outgoing = permute(flat, slot_list[None, :], cut)
    else:
        in_slots = permute(flat, slot_list[None, :], flat.shape)
        outgoing = in_slots.reshape(levels, targets, per_target).transpose(1, 0, 2)
    crm_moisture, outgoing = lax.optimization_barrier((crm_moisture, outgoing))
    arrived = lax.all_to_all(outgoing, ("sec", "lat"), split_axis=0, concat_axis=0, tiled=True)
    homeward = cloud_model(arrived, crm_moisture[0, :, :, 0, 0, :], sections)
    returned = lax.all_to_all(homeward, ("sec", "lat"), split_axis=0, concat_axis=0, tiled=True)
    if not tiled:
        returned = returned.transpose(1, 0, 2).reshape(levels, block_cols)
    rainfall = permute(returned, inverse_order(slot_list)[None, :], flat.shape)
    rainfall = rainfall.reshape(levels, band_rows, lon_block)
    share = jnp.where(
        field < 2, own * (-1.0 / NSUB), jnp.where(field == 2, jnp.float32(1), jnp.float32(-1))
    )
    fresh = own + (share * rainfall + force)

    regrouped = lax.all_to_all(fresh, "col", split_axis=0, concat_axis=0, tiled=True)
    owner_count = MMAX // lat_bands
    wave_table, _ = lax.optimization_barrier((wave_table, rainfall))
    owned_waves = lax.dynamic_slice_in_dim(
        wave_table, lax.axis_index("lat") * owner_count, owner_count
    )
    tables = legendre_tables(owned_waves, NLAT, lat_bands)
    regrouped, tables = lax.optimization_barrier((regrouped, tables))
    spectra = dft(regrouped, wave_table, lax.axis_size("col"), lat_bands)
    gathered = lax.all_to_all(spectra, "lat", split_axis=0, concat_axis=0, tiled=True)
    coeffs = contract_tables(gathered, tables)
    return (fresh[None, None], coeffs[None, None])


def solution(mesh):
    placed = (
        P(None, "sec", None, "lat", "col"),
        P(None, "sec", None, "lat", "col"),
        P(None, None, None, ("sec", "lat"), "col", None),
        P("col", "lat", None),
        P(),
    )
    return jax.shard_map(
        shards,
        mesh=mesh,
        in_specs=placed,
        out_specs=(P(None, "sec", None, "lat", "col"), P("sec", None, "col", "lat", None, None)),
        check_vma=False,
    )
```

```python
import math

import jax
import jax.numpy as jnp
from jax import lax
from jax.experimental import pallas as pl
from jax.experimental.pallas import tpu as pltpu
from jax.sharding import PartitionSpec as P

NLON = 384
NLAT = 192
MMAX = 128
NSUB = 4
LANES = 128
ROWS = 8

COURANT_SCALE = 0.4
CONDENSE = 0.5


def permute_kernel(x_ref, order_ref, *refs):
    *updates, out_ref, parts, held = refs
    levels = x_ref.shape[-2]
    rows = held.shape[0]
    cols = order_ref.shape[1]
    tiles = cols // LANES
    gathered = held.shape[1] // LANES
    multiplied = tiles - gathered
    halves = 2 if tiles % 2 == 0 else 1
    width = halves * LANES
    fill = jnp.zeros((rows - levels, LANES), jnp.float32)
    groups = range(rows // ROWS)

    for s in range(tiles):
        if x_ref.ndim == 2:
            block = x_ref[:, s * LANES : (s + 1) * LANES]
        else:
            per = x_ref.shape[2] // LANES
            block = x_ref[s // per, :, s % per * LANES : (s % per + 1) * LANES]
        if rows > levels:
            block = jnp.concatenate([block, fill], axis=0)
        if s < multiplied:
            coarse = block.astype(jnp.bfloat16)
            parts[s * rows : (s + 1) * rows, :LANES] = coarse
            parts[s * rows : (s + 1) * rows, LANES:] = (
                block - coarse.astype(jnp.float32)
            ).astype(jnp.bfloat16)
        else:
            held[:, (s - multiplied) * LANES : (s - multiplied + 1) * LANES] = block
    wanted = lax.broadcasted_iota(jnp.int32, (2 * LANES, width), 0) & (LANES - 1)

    def one(t, carry):
        order = order_ref[:, pl.ds(pl.multiple_of(t * width, width), width)]
        lane = order & (LANES - 1)
        chosen = jnp.where(wanted == lane, 1.0, 0.0).astype(jnp.bfloat16)
        moved = jnp.dot(parts[...], chosen, preferred_element_type=jnp.float32)
        for h in range(halves):
            mine = slice(h * LANES, (h + 1) * LANES)
            source = jnp.broadcast_to(order[:, mine] >> 7, (ROWS, LANES))
            lanes = jnp.broadcast_to(lane[:, mine], (ROWS, LANES))
            total = [jnp.zeros((ROWS, LANES), jnp.float32) for _ in groups]
            for s in range(gathered):
                hit = source == multiplied + s
                for r in groups:
                    block = held[r * ROWS : (r + 1) * ROWS, s * LANES : (s + 1) * LANES]
                    total[r] = jnp.where(hit, jnp.take_along_axis(block, lanes, axis=1), total[r])
            for s in range(multiplied):
                hit = source == s
                for r in groups:
                    begin = s * rows + r * ROWS
                    total[r] = jnp.where(hit, moved[begin : begin + ROWS, mine], total[r])
            tile = t * halves + h
            for r in groups:
                end = min((r + 1) * ROWS, levels)
                value = total[r][: end - r * ROWS]
                if out_ref.ndim == 2:
                    at = pl.ds(pl.multiple_of(tile * LANES, LANES), LANES)
                    if updates:
                        share_ref, base_ref = updates
                        value = base_ref[r * ROWS : end, at] + share_ref[r * ROWS : end, at] * value
                    out_ref[r * ROWS : end, at] = value
                else:
                    per = out_ref.shape[2] // LANES
                    at = pl.ds(pl.multiple_of(tile % per * LANES, LANES), LANES)
                    out_ref[tile // per, r * ROWS : end, at] = value
        return carry

    lax.fori_loop(0, tiles // halves, one, 0)


def permute(values, order, shape, updates=()):
    levels, tiles = values.shape[-2], order.shape[1] // LANES
    rows = -(-levels // ROWS) * ROWS
    gathered = tiles * 3 // 8
    return pl.pallas_call(
        permute_kernel,
        out_shape=jax.ShapeDtypeStruct(shape, jnp.float32),
        in_specs=[pl.BlockSpec(memory_space=pltpu.VMEM)] * (2 + len(updates)),
        out_specs=pl.BlockSpec(memory_space=pltpu.VMEM),
        scratch_shapes=[
            pltpu.VMEM(((tiles - gathered) * rows, 2 * LANES), jnp.bfloat16),
            pltpu.VMEM((rows, gathered * LANES), jnp.float32),
        ],
        name="permute",
    )(values, order, *updates)


def cloud_kernel(wind_ref, gap_ref, push_ref, anomaly_ref, rain_ref):
    count, levels, width = anomaly_ref.shape
    scale = CONDENSE / count

    for c0 in range(0, width, LANES):
        c1 = min(c0 + LANES, width)
        for base in range(0, levels, 2 * ROWS):
            top = min(base + 2 * ROWS, levels)
            for r0 in range(base, top, ROWS):
                r1 = min(r0 + ROWS, top)
                courant = COURANT_SCALE * jnp.tanh(wind_ref[r0:r1, c0:c1])
                mixing = 0.2 + 0.5 * jnp.abs(courant)
                ahead = mixing - 0.5 * courant
                back = mixing + 0.5 * courant
                keep = 1.0 - 2.0 * mixing
                push = push_ref[r0:r1, c0:c1]
                start = gap_ref[r0:r1, c0:c1]
                gap = [
                    start
                    + anomaly_ref[n, base:top, c0:c1].astype(jnp.float32)[r0 - base : r1 - base]
                    for n in range(count)
                ]
                rain = [jnp.zeros_like(start) for _ in range(2)]
                for substep in range(NSUB):
                    fresh = []
                    for n in range(count):
                        wet = jnp.maximum(gap[n], 0.0)
                        rain[n % 2] = rain[n % 2] + wet
                        if substep < NSUB - 1:
                            fresh.append(
                                (ahead * gap[(n + 1) % count] + back * gap[n - 1])
                                + (keep * gap[n] + (push - wet))
                            )
                    gap = fresh
                found = scale * (rain[0] + rain[1])
                for copy in range(rain_ref.shape[0]):
                    rain_ref[copy, r0:r1, c0:c1] = found


def cloud_model(arrived, anomaly, sections):
    count, levels, _ = anomaly.shape
    blocks, _, span = arrived.shape
    bands = blocks // sections
    block = LANES if span % LANES == 0 else span
    steps = span // block
    if block < LANES:
        anomaly = anomaly.reshape(count, levels, bands, span).transpose(2, 0, 1, 3)
        moist = pl.BlockSpec((None, count, levels, span), lambda i: (i, 0, 0, 0))
    else:
        moist = pl.BlockSpec((count, levels, block), lambda i: (0, 0, i))

    def of(field):
        return pl.BlockSpec(
            (None, levels, block), lambda i: (field * bands + i // steps, 0, i % steps)
        )

    found = pl.pallas_call(
        cloud_kernel,
        grid=(bands * steps,),
        out_shape=jax.ShapeDtypeStruct((sections, bands, levels, span), jnp.float32),
        in_specs=[of(0), of(2), of(3), moist],
        out_specs=pl.BlockSpec(
            (sections, None, levels, block), lambda i: (0, i // steps, 0, i % steps)
        ),
        name="cloud",
    )(arrived, arrived, arrived, anomaly)
    return found.reshape(arrived.shape)


def halve(values):
    coarse = values.astype(jnp.bfloat16)
    return coarse, (values - coarse.astype(jnp.float32)).astype(jnp.bfloat16)


def march_kernel(
    grow_ref, retreat_ref, order_ref, zero_ref, cosine_ref, diag_ref, coarse_ref, fine_ref, *tables
):
    slots = order_ref.shape[0]
    halves = len(tables)
    order = order_ref[...]
    grow = grow_ref[...]
    retreat = retreat_ref[...]
    cosine = [cosine_ref[:, h * LANES : (h + 1) * LANES] for h in range(halves)]
    for h in range(halves):
        tables[h][: 2 * slots, :] = jnp.zeros((2 * slots, LANES), jnp.float32)
    group = 8

    def march(g, carry):
        begin = g * group
        held = [
            [
                tables[h][pl.ds(pl.multiple_of((begin + j) * slots, ROWS), slots), :]
                for j in range(2)
            ]
            for h in range(halves)
        ]
        for j in range(group):
            n = begin + j
            index = zero_ref[...] + n
            grow_n = jnp.take_along_axis(grow, index, axis=1)
            retreat_n = jnp.take_along_axis(retreat, index, axis=1)
            first = order == n
            for h in range(halves):
                previous, current = held[h]
                grown = grow_n * (cosine[h] * current - retreat_n * previous)
                fresh = jnp.where(first, diag_ref[:, h * LANES : (h + 1) * LANES], grown)
                tables[h][pl.ds(pl.multiple_of((n + 2) * slots, ROWS), slots), :] = fresh
                held[h] = [current, fresh]
        return carry

    lax.fori_loop(0, MMAX // group, march, 0)

    def sort(g, carry):
        for j in range(4):
            s = g * 4 + j
            for h in range(halves):
                rows = tables[h][pl.ds(2 * slots + s, MMAX, stride=slots), :]
                mine = slice(h * LANES, (h + 1) * LANES)
                coarse_ref[s, :, mine], fine_ref[s, :, mine] = halve(rows)
        return carry

    lax.fori_loop(0, slots // 4, sort, 0)


def contract_kernel(fourier_ref, coarse_ref, fine_ref, out_ref):
    levels, share, _, _ = out_ref.shape
    bands = fourier_ref.shape[0]
    terms = 2 * levels
    slots = fourier_ref.shape[1] // terms
    begin = pl.program_id(0) * share
    rows = -(-terms // 16) * 16

    def product(left, right):
        return lax.dot_general(
            left, right, (((1,), (1,)), ((), ())), preferred_element_type=jnp.float32
        )

    def contract(g, carry):
        for j in range(4):
            s = g * 4 + j
            found = [fourier_ref[b, pl.ds(begin + s, terms, stride=slots), :] for b in range(bands)]
            found = jnp.concatenate(found, axis=1)
            if rows > terms:
                fill = jnp.zeros((rows - terms, found.shape[1]), jnp.float32)
                found = jnp.concatenate([found, fill], axis=0)
            head, rest = halve(found)
            main = product(jnp.concatenate([head, rest], axis=0), coarse_ref[s])
            total = main[:rows] + main[rows:] + product(head, fine_ref[s])
            for l in range(levels):
                out_ref[l, s] = total[2 * l : 2 * l + 2]
        return carry

    lax.fori_loop(0, share // 4, contract, 0)


def dft_kernel(x_ref, trig_ref, out_ref):
    blocks, levels, lats, _ = x_ref.shape
    parts, _, _, slots, lanes = out_ref.shape
    count = trig_ref.shape[1]
    waves = [jnp.concatenate(halve(trig_ref[j]), axis=0) for j in range(blocks)]

    def product(left, right):
        return lax.dot_general(
            left, right, (((1,), (1,)), ((), ())), preferred_element_type=jnp.float32
        )

    for first in range(0, levels, 2):
        last = min(first + 2, levels)
        total = None
        for j in range(blocks):
            grid = []
            for l in range(first, last):
                grid.append(x_ref[j, l])
                if lanes > lats:
                    grid.append(jnp.zeros((lanes - lats, x_ref.shape[3]), jnp.float32))
            coarse, fine = halve(jnp.concatenate(grid, axis=0))
            main = product(waves[j], coarse)
            term = main[:count] + main[count:] + product(waves[j][:count], fine)
            total = term if total is None else total + term
        for l in range(first, last):
            mine = total[:, (l - first) * lanes : (l - first + 1) * lanes]
            for p in range(parts):
                for c in range(2):
                    begin = (p * 2 + c) * slots
                    out_ref[p, l, c] = mine[begin : begin + slots]


def dft(regrouped, wave_table, blocks, parts):
    _, lats, lons = regrouped.shape
    levels = regrouped.shape[0] // blocks
    slots = wave_table.shape[0] // parts
    pad = -lats % ROWS
    lanes = -(-lats // LANES) * LANES
    grid = jnp.pad(regrouped, ((0, 0), (0, pad), (0, 0)))
    trig = trig_table(jnp.arange(NLON, dtype=jnp.int32), wave_table)
    trig = trig.reshape(blocks, lons, 2, parts, slots).transpose(0, 3, 2, 4, 1)
    return pl.pallas_call(
        dft_kernel,
        out_shape=jax.ShapeDtypeStruct((parts, levels, 2, slots, lanes), jnp.float32),
        in_specs=[pl.BlockSpec(memory_space=pltpu.VMEM)] * 2,
        out_specs=pl.BlockSpec(memory_space=pltpu.VMEM),
        name="dft",
    )(
        grid.reshape(blocks, levels, lats + pad, lons),
        trig.reshape(blocks, 2 * parts * slots, lons),
    )


def legendre_tables(orders, lats, bands):
    slots = orders.shape[0]
    wide = bands * (-(-(lats // bands) // LANES) * LANES)
    colatitude = (jnp.arange(lats, dtype=jnp.int32).astype(jnp.float32) + 0.5) * (math.pi / lats)
    sine_lat = jnp.sin(colatitude)
    order_col = orders.astype(jnp.float32)[:, None]
    log_diag = 0.5 * (
        lax.lgamma(order_col + 1.5) - lax.lgamma(jnp.float32(1.5)) - lax.lgamma(order_col + 1.0)
    )
    log_diag = log_diag + order_col * jnp.log(sine_lat)[None, :] - 0.5 * math.log(2.0)
    diagonal = jnp.exp(log_diag) * (sine_lat / math.sqrt(lats))[None, :]
    degree = jnp.arange(MMAX, dtype=jnp.int32).astype(jnp.float32)[None, :]
    active = degree > order_col
    numerator = jnp.where(active, 4.0 * degree * degree - 1.0, 0.0)
    bottom = jnp.where(active, degree * degree - order_col * order_col, 1.0)
    lower = degree - 1.0
    retreat = jnp.sqrt(
        jnp.maximum(lower * lower - order_col * order_col, 0.0) / (4.0 * lower * lower - 1.0)
    )
    grow = jnp.sqrt(numerator / bottom)

    def spread(values):
        cut = values.reshape(values.shape[0], bands, lats // bands)
        cut = jnp.pad(cut, ((0, 0), (0, 0), (0, wide // bands - lats // bands)))
        return cut.reshape(values.shape[0], wide)

    table = jax.ShapeDtypeStruct((slots, MMAX, wide), jnp.bfloat16)
    return pl.pallas_call(
        march_kernel,
        out_shape=[table] * 2,
        in_specs=[pl.BlockSpec(memory_space=pltpu.VMEM)] * 6,
        out_specs=[pl.BlockSpec(memory_space=pltpu.VMEM)] * 2,
        scratch_shapes=[pltpu.VMEM(((MMAX + 2) * slots, LANES), jnp.float32)] * (wide // LANES),
        cost_estimate=pl.CostEstimate(
            flops=6 * MMAX * slots * wide, bytes_accessed=16 * MMAX * slots * wide, transcendentals=0
        ),
        name="march",
    )(
        grow,
        retreat,
        jnp.broadcast_to(orders[:, None], (slots, LANES)),
        jnp.zeros((slots, LANES), jnp.int32),
        spread(jnp.cos(colatitude)[None, :]),
        spread(diagonal),
    )


def contract_tables(fourier, tables):
    bands, levels, _, slots, lanes = fourier.shape
    step = 8
    rows = levels * 2 * slots
    table = pl.BlockSpec((step, MMAX, bands * lanes), lambda i: (i, 0, 0))
    return pl.pallas_call(
        contract_kernel,
        grid=(slots // step,),
        out_shape=jax.ShapeDtypeStruct((levels, slots, 2, MMAX), jnp.float32),
        in_specs=[pl.BlockSpec((bands, rows, lanes), lambda i: (0, 0, 0)), table, table],
        out_specs=pl.BlockSpec((levels, step, 2, MMAX), lambda i: (0, i, 0, 0)),
        name="contract",
    )(fourier.reshape(bands, levels * 2 * slots, lanes), *tables)


def trig_table(longitudes, wave_numbers):
    phase = (longitudes[:, None] * wave_numbers[None, :] % NLON).astype(jnp.float32) * (
        2.0 * math.pi / NLON
    )
    return jnp.stack((jnp.cos(phase), jnp.sin(phase)), axis=1) / math.sqrt(NLON)


def inverse_order(order):
    cols = order.shape[0]
    tiles = cols // LANES
    slots = jnp.arange(cols, dtype=jnp.int32)
    high = (order[None, :] // LANES) == jnp.arange(tiles, dtype=jnp.int32)[:, None]
    low = (order[:, None] % LANES) == jnp.arange(LANES, dtype=jnp.int32)[None, :]
    digits = jnp.stack((slots // LANES, slots % LANES)).astype(jnp.bfloat16)
    left = jnp.where(high[None], digits[:, None, :], jnp.bfloat16(0)).reshape(2 * tiles, cols)
    found = jnp.dot(left, low.astype(jnp.bfloat16), preferred_element_type=jnp.float32)
    found = found.reshape(2, cols).astype(jnp.int32)
    return found[0] * LANES + found[1]


def shards(state, forcing, crm_moisture, cloud_order, wave_table):
    members, _, levels, band_rows, lon_block = state.shape
    sections = lax.axis_size("sec")
    lat_bands = lax.axis_size("lat")
    block_cols = band_rows * lon_block
    targets = sections * lat_bands
    per_target = block_cols // targets
    field = lax.axis_index("sec")
    slot_list = cloud_order[0, 0]
    own, force = state[0, 0], forcing[0, 0]

    mate = lax.ppermute(jnp.where(field == 2, force, own), "sec", [(2, 3), (3, 2)])
    part = jnp.where(
        field == 3, (force - mate) / NSUB, jnp.where(field == 2, mate - own, own)
    )
    flat = part.reshape(levels, block_cols)
    cut = (targets, levels, per_target)
    tiled = per_target % LANES == 0
    if tiled:
        outgoing = permute(flat, slot_list[None, :], cut)
    else:
        in_slots = permute(flat, slot_list[None, :], flat.shape)
        outgoing = in_slots.reshape(levels, targets, per_target).transpose(1, 0, 2)
    crm_moisture, outgoing, own, force = lax.optimization_barrier(
        (crm_moisture, outgoing, own, force)
    )
    share = jnp.where(
        field < 2, own * (-1.0 / NSUB), jnp.where(field == 2, jnp.float32(1), jnp.float32(-1))
    ).reshape(flat.shape)
    base = (own + force).reshape(flat.shape)
    arrived = lax.all_to_all(outgoing, ("sec", "lat"), split_axis=0, concat_axis=0, tiled=True)
    homeward = cloud_model(arrived, crm_moisture[0, :, :, 0, 0, :], sections)
    returned = lax.all_to_all(homeward, ("sec", "lat"), split_axis=0, concat_axis=0, tiled=True)
    if not tiled:
        returned = returned.transpose(1, 0, 2).reshape(levels, block_cols)
    fresh = permute(returned, inverse_order(slot_list)[None, :], flat.shape, (share, base))
    fresh = fresh.reshape(levels, band_rows, lon_block)

    regrouped = lax.all_to_all(fresh, "col", split_axis=0, concat_axis=0, tiled=True)
    owner_count = MMAX // lat_bands
    wave_table, _ = lax.optimization_barrier((wave_table, fresh))
    owned_waves = lax.dynamic_slice_in_dim(
        wave_table, lax.axis_index("lat") * owner_count, owner_count
    )
    tables = legendre_tables(owned_waves, NLAT, lat_bands)
    regrouped, tables = lax.optimization_barrier((regrouped, tables))
    spectra = dft(regrouped, wave_table, lax.axis_size("col"), lat_bands)
    gathered = lax.all_to_all(spectra, "lat", split_axis=0, concat_axis=0, tiled=True)
    coeffs = contract_tables(gathered, tables)
    return (fresh[None, None], coeffs[None, None])


def solution(mesh):
    placed = (
        P(None, "sec", None, "lat", "col"),
        P(None, "sec", None, "lat", "col"),
        P(None, None, None, ("sec", "lat"), "col", None),
        P("col", "lat", None),
        P(),
    )
    return jax.shard_map(
        shards,
        mesh=mesh,
        in_specs=placed,
        out_specs=(P(None, "sec", None, "lat", "col"), P("sec", None, "col", "lat", None, None)),
        check_vma=False,
    )
```

```python
import math

import jax
import jax.numpy as jnp
from jax import lax
from jax.experimental import pallas as pl
from jax.experimental.pallas import tpu as pltpu
from jax.sharding import PartitionSpec as P

NLON = 384
NLAT = 192
MMAX = 128
NSUB = 4
LANES = 128
ROWS = 8

COURANT_SCALE = 0.4
CONDENSE = 0.5


def permute_kernel(x_ref, order_ref, out_ref, parts, held):
    levels = x_ref.shape[-2]
    rows = held.shape[0]
    cols = order_ref.shape[1]
    tiles = cols // LANES
    gathered = held.shape[1] // LANES
    multiplied = tiles - gathered
    halves = 2 if tiles % 2 == 0 else 1
    width = halves * LANES
    fill = jnp.zeros((rows - levels, LANES), jnp.float32)
    groups = range(rows // ROWS)

    for s in range(tiles):
        if x_ref.ndim == 2:
            block = x_ref[:, s * LANES : (s + 1) * LANES]
        else:
            per = x_ref.shape[2] // LANES
            block = x_ref[s // per, :, s % per * LANES : (s % per + 1) * LANES]
        if rows > levels:
            block = jnp.concatenate([block, fill], axis=0)
        if s < multiplied:
            coarse = block.astype(jnp.bfloat16)
            parts[s * rows : (s + 1) * rows, :LANES] = coarse
            parts[s * rows : (s + 1) * rows, LANES:] = (
                block - coarse.astype(jnp.float32)
            ).astype(jnp.bfloat16)
        else:
            held[:, (s - multiplied) * LANES : (s - multiplied + 1) * LANES] = block
    wanted = lax.broadcasted_iota(jnp.int32, (2 * LANES, width), 0) & (LANES - 1)

    def one(t, carry):
        order = order_ref[:, pl.ds(pl.multiple_of(t * width, width), width)]
        lane = order & (LANES - 1)
        chosen = jnp.where(wanted == lane, 1.0, 0.0).astype(jnp.bfloat16)
        moved = jnp.dot(parts[...], chosen, preferred_element_type=jnp.float32)
        for h in range(halves):
            mine = slice(h * LANES, (h + 1) * LANES)
            source = jnp.broadcast_to(order[:, mine] >> 7, (ROWS, LANES))
            lanes = jnp.broadcast_to(lane[:, mine], (ROWS, LANES))
            total = [jnp.zeros((ROWS, LANES), jnp.float32) for _ in groups]
            for s in range(gathered):
                hit = source == multiplied + s
                for r in groups:
                    block = held[r * ROWS : (r + 1) * ROWS, s * LANES : (s + 1) * LANES]
                    total[r] = jnp.where(hit, jnp.take_along_axis(block, lanes, axis=1), total[r])
            for s in range(multiplied):
                hit = source == s
                for r in groups:
                    begin = s * rows + r * ROWS
                    total[r] = jnp.where(hit, moved[begin : begin + ROWS, mine], total[r])
            tile = t * halves + h
            for r in groups:
                end = min((r + 1) * ROWS, levels)
                value = total[r][: end - r * ROWS]
                if out_ref.ndim == 2:
                    at = pl.ds(pl.multiple_of(tile * LANES, LANES), LANES)
                    out_ref[r * ROWS : end, at] = value
                else:
                    per = out_ref.shape[2] // LANES
                    at = pl.ds(pl.multiple_of(tile % per * LANES, LANES), LANES)
                    out_ref[tile // per, r * ROWS : end, at] = value
        return carry

    lax.fori_loop(0, tiles // halves, one, 0)


def permute(values, order, shape):
    levels, tiles = values.shape[-2], order.shape[1] // LANES
    rows = -(-levels // ROWS) * ROWS
    gathered = tiles * 7 // 16
    return pl.pallas_call(
        permute_kernel,
        out_shape=jax.ShapeDtypeStruct(shape, jnp.float32),
        in_specs=[pl.BlockSpec(memory_space=pltpu.VMEM)] * 2,
        out_specs=pl.BlockSpec(memory_space=pltpu.VMEM),
        scratch_shapes=[
            pltpu.VMEM(((tiles - gathered) * rows, 2 * LANES), jnp.bfloat16),
            pltpu.VMEM((rows, gathered * LANES), jnp.float32),
        ],
        name="permute",
    )(values, order)


def cloud_kernel(wind_ref, gap_ref, push_ref, anomaly_ref, rain_ref):
    count, levels, width = anomaly_ref.shape
    scale = CONDENSE / count

    for c0 in range(0, width, LANES):
        c1 = min(c0 + LANES, width)
        for base in range(0, levels, 2 * ROWS):
            top = min(base + 2 * ROWS, levels)
            for r0 in range(base, top, ROWS):
                r1 = min(r0 + ROWS, top)
                courant = COURANT_SCALE * jnp.tanh(wind_ref[r0:r1, c0:c1])
                mixing = 0.2 + 0.5 * jnp.abs(courant)
                ahead = mixing - 0.5 * courant
                back = mixing + 0.5 * courant
                keep = 1.0 - 2.0 * mixing
                push = push_ref[r0:r1, c0:c1]
                start = gap_ref[r0:r1, c0:c1]
                gap = [
                    start
                    + anomaly_ref[n, base:top, c0:c1].astype(jnp.float32)[r0 - base : r1 - base]
                    for n in range(count)
                ]
                rain = [jnp.zeros_like(start) for _ in range(2)]
                for substep in range(NSUB):
                    fresh = []
                    for n in range(count):
                        wet = jnp.maximum(gap[n], 0.0)
                        rain[n % 2] = rain[n % 2] + wet
                        if substep < NSUB - 1:
                            fresh.append(
                                (ahead * gap[(n + 1) % count] + back * gap[n - 1])
                                + (keep * gap[n] + (push - wet))
                            )
                    gap = fresh
                found = scale * (rain[0] + rain[1])
                for copy in range(rain_ref.shape[0]):
                    rain_ref[copy, r0:r1, c0:c1] = found


def cloud_model(arrived, anomaly, sections):
    count, levels, _ = anomaly.shape
    blocks, _, span = arrived.shape
    bands = blocks // sections
    block = LANES if span % LANES == 0 else span
    steps = span // block
    if block < LANES:
        anomaly = anomaly.reshape(count, levels, bands, span).transpose(2, 0, 1, 3)
        moist = pl.BlockSpec((None, count, levels, span), lambda i: (i, 0, 0, 0))
    else:
        moist = pl.BlockSpec((count, levels, block), lambda i: (0, 0, i))

    def of(field):
        return pl.BlockSpec(
            (None, levels, block), lambda i: (field * bands + i // steps, 0, i % steps)
        )

    found = pl.pallas_call(
        cloud_kernel,
        grid=(bands * steps,),
        out_shape=jax.ShapeDtypeStruct((sections, bands, levels, span), jnp.float32),
        in_specs=[of(0), of(2), of(3), moist],
        out_specs=pl.BlockSpec(
            (sections, None, levels, block), lambda i: (0, i // steps, 0, i % steps)
        ),
        name="cloud",
    )(arrived, arrived, arrived, anomaly)
    return found.reshape(arrived.shape)


def halve(values):
    coarse = values.astype(jnp.bfloat16)
    return coarse, (values - coarse.astype(jnp.float32)).astype(jnp.bfloat16)


def march_kernel(
    grow_ref, retreat_ref, order_ref, zero_ref, cosine_ref, diag_ref, coarse_ref, fine_ref, *tables
):
    slots = order_ref.shape[0]
    halves = len(tables)
    order = order_ref[...]
    grow = grow_ref[...]
    retreat = retreat_ref[...]
    cosine = [cosine_ref[:, h * LANES : (h + 1) * LANES] for h in range(halves)]
    for h in range(halves):
        tables[h][: 2 * slots, :] = jnp.zeros((2 * slots, LANES), jnp.float32)
    group = 8

    def march(g, carry):
        begin = g * group
        held = [
            [
                tables[h][pl.ds(pl.multiple_of((begin + j) * slots, ROWS), slots), :]
                for j in range(2)
            ]
            for h in range(halves)
        ]
        for j in range(group):
            n = begin + j
            index = zero_ref[...] + n
            grow_n = jnp.take_along_axis(grow, index, axis=1)
            retreat_n = jnp.take_along_axis(retreat, index, axis=1)
            first = order == n
            for h in range(halves):
                previous, current = held[h]
                grown = grow_n * (cosine[h] * current - retreat_n * previous)
                fresh = jnp.where(first, diag_ref[:, h * LANES : (h + 1) * LANES], grown)
                tables[h][pl.ds(pl.multiple_of((n + 2) * slots, ROWS), slots), :] = fresh
                held[h] = [current, fresh]
        return carry

    lax.fori_loop(0, MMAX // group, march, 0)

    def sort(g, carry):
        for j in range(4):
            s = g * 4 + j
            for h in range(halves):
                rows = tables[h][pl.ds(2 * slots + s, MMAX, stride=slots), :]
                mine = slice(h * LANES, (h + 1) * LANES)
                coarse_ref[s, :, mine], fine_ref[s, :, mine] = halve(rows)
        return carry

    lax.fori_loop(0, slots // 4, sort, 0)


def contract_kernel(fourier_ref, coarse_ref, fine_ref, out_ref):
    levels, slots, _, _ = out_ref.shape
    bands = fourier_ref.shape[0]
    terms = 2 * levels
    rows = -(-terms // 16) * 16

    def product(left, right):
        return lax.dot_general(
            left, right, (((1,), (1,)), ((), ())), preferred_element_type=jnp.float32
        )

    def contract(g, carry):
        for j in range(4):
            s = g * 4 + j
            found = [fourier_ref[b, pl.ds(s, terms, stride=slots), :] for b in range(bands)]
            found = jnp.concatenate(found, axis=1)
            if rows > terms:
                fill = jnp.zeros((rows - terms, found.shape[1]), jnp.float32)
                found = jnp.concatenate([found, fill], axis=0)
            head, rest = halve(found)
            main = product(jnp.concatenate([head, rest], axis=0), coarse_ref[s])
            total = main[:rows] + main[rows:] + product(head, fine_ref[s])
            for l in range(levels):
                out_ref[l, s] = total[2 * l : 2 * l + 2]
        return carry

    lax.fori_loop(0, slots // 4, contract, 0)


def dft_kernel(x_ref, trig_ref, out_ref):
    blocks, levels, lats, _ = x_ref.shape
    parts, _, _, slots, lanes = out_ref.shape
    count = trig_ref.shape[1]
    waves = [jnp.concatenate(halve(trig_ref[j]), axis=0) for j in range(blocks)]

    def product(left, right):
        return lax.dot_general(
            left, right, (((1,), (1,)), ((), ())), preferred_element_type=jnp.float32
        )

    for first in range(0, levels, 2):
        last = min(first + 2, levels)
        total = None
        for j in range(blocks):
            grid = []
            for l in range(first, last):
                grid.append(x_ref[j, l])
                if lanes > lats:
                    grid.append(jnp.zeros((lanes - lats, x_ref.shape[3]), jnp.float32))
            coarse, fine = halve(jnp.concatenate(grid, axis=0))
            main = product(waves[j], coarse)
            term = main[:count] + main[count:] + product(waves[j][:count], fine)
            total = term if total is None else total + term
        for l in range(first, last):
            mine = total[:, (l - first) * lanes : (l - first + 1) * lanes]
            for p in range(parts):
                for c in range(2):
                    begin = (p * 2 + c) * slots
                    out_ref[p, l, c] = mine[begin : begin + slots]


def dft(regrouped, wave_table, blocks, parts):
    _, lats, lons = regrouped.shape
    levels = regrouped.shape[0] // blocks
    slots = wave_table.shape[0] // parts
    pad = -lats % ROWS
    lanes = -(-lats // LANES) * LANES
    grid = jnp.pad(regrouped, ((0, 0), (0, pad), (0, 0)))
    trig = trig_table(jnp.arange(NLON, dtype=jnp.int32), wave_table)
    trig = trig.reshape(blocks, lons, 2, parts, slots).transpose(0, 3, 2, 4, 1)
    return pl.pallas_call(
        dft_kernel,
        out_shape=jax.ShapeDtypeStruct((parts, levels, 2, slots, lanes), jnp.float32),
        in_specs=[pl.BlockSpec(memory_space=pltpu.VMEM)] * 2,
        out_specs=pl.BlockSpec(memory_space=pltpu.VMEM),
        name="dft",
    )(
        grid.reshape(blocks, levels, lats + pad, lons),
        trig.reshape(blocks, 2 * parts * slots, lons),
    )


def legendre_tables(orders, lats, bands):
    slots = orders.shape[0]
    wide = bands * (-(-(lats // bands) // LANES) * LANES)
    colatitude = (jnp.arange(lats, dtype=jnp.int32).astype(jnp.float32) + 0.5) * (math.pi / lats)
    sine_lat = jnp.sin(colatitude)
    order_col = orders.astype(jnp.float32)[:, None]
    log_diag = 0.5 * (
        lax.lgamma(order_col + 1.5) - lax.lgamma(jnp.float32(1.5)) - lax.lgamma(order_col + 1.0)
    )
    log_diag = log_diag + order_col * jnp.log(sine_lat)[None, :] - 0.5 * math.log(2.0)
    diagonal = jnp.exp(log_diag) * (sine_lat / math.sqrt(lats))[None, :]
    degree = jnp.arange(MMAX, dtype=jnp.int32).astype(jnp.float32)[None, :]
    active = degree > order_col
    numerator = jnp.where(active, 4.0 * degree * degree - 1.0, 0.0)
    bottom = jnp.where(active, degree * degree - order_col * order_col, 1.0)
    lower = degree - 1.0
    retreat = jnp.sqrt(
        jnp.maximum(lower * lower - order_col * order_col, 0.0) / (4.0 * lower * lower - 1.0)
    )
    grow = jnp.sqrt(numerator / bottom)

    def spread(values):
        cut = values.reshape(values.shape[0], bands, lats // bands)
        cut = jnp.pad(cut, ((0, 0), (0, 0), (0, wide // bands - lats // bands)))
        return cut.reshape(values.shape[0], wide)

    table = jax.ShapeDtypeStruct((slots, MMAX, wide), jnp.bfloat16)
    return pl.pallas_call(
        march_kernel,
        out_shape=[table] * 2,
        in_specs=[pl.BlockSpec(memory_space=pltpu.VMEM)] * 6,
        out_specs=[pl.BlockSpec(memory_space=pltpu.VMEM)] * 2,
        scratch_shapes=[pltpu.VMEM(((MMAX + 2) * slots, LANES), jnp.float32)] * (wide // LANES),
        cost_estimate=pl.CostEstimate(
            flops=6 * MMAX * slots * wide, bytes_accessed=16 * MMAX * slots * wide, transcendentals=0
        ),
        name="march",
    )(
        grow,
        retreat,
        jnp.broadcast_to(orders[:, None], (slots, LANES)),
        jnp.zeros((slots, LANES), jnp.int32),
        spread(jnp.cos(colatitude)[None, :]),
        spread(diagonal),
    )


def contract_tables(fourier, tables):
    bands, levels, _, slots, lanes = fourier.shape
    return pl.pallas_call(
        contract_kernel,
        out_shape=jax.ShapeDtypeStruct((levels, slots, 2, MMAX), jnp.float32),
        in_specs=[pl.BlockSpec(memory_space=pltpu.VMEM)] * 3,
        out_specs=pl.BlockSpec(memory_space=pltpu.VMEM),
        name="contract",
    )(fourier.reshape(bands, levels * 2 * slots, lanes), *tables)


def trig_table(longitudes, wave_numbers):
    phase = (longitudes[:, None] * wave_numbers[None, :] % NLON).astype(jnp.float32) * (
        2.0 * math.pi / NLON
    )
    return jnp.stack((jnp.cos(phase), jnp.sin(phase)), axis=1) / math.sqrt(NLON)


def inverse_order(order):
    cols = order.shape[0]
    tiles = cols // LANES
    slots = jnp.arange(cols, dtype=jnp.int32)
    high = (order[None, :] // LANES) == jnp.arange(tiles, dtype=jnp.int32)[:, None]
    low = (order[:, None] % LANES) == jnp.arange(LANES, dtype=jnp.int32)[None, :]
    digits = jnp.stack((slots // LANES, slots % LANES)).astype(jnp.bfloat16)
    left = jnp.where(high[None], digits[:, None, :], jnp.bfloat16(0)).reshape(2 * tiles, cols)
    found = jnp.dot(left, low.astype(jnp.bfloat16), preferred_element_type=jnp.float32)
    found = found.reshape(2, cols).astype(jnp.int32)
    return found[0] * LANES + found[1]


def shards(state, forcing, crm_moisture, cloud_order, wave_table):
    members, _, levels, band_rows, lon_block = state.shape
    sections = lax.axis_size("sec")
    lat_bands = lax.axis_size("lat")
    block_cols = band_rows * lon_block
    targets = sections * lat_bands
    per_target = block_cols // targets
    field = lax.axis_index("sec")
    slot_list = cloud_order[0, 0]
    own, force = state[0, 0], forcing[0, 0]

    mate = lax.ppermute(jnp.where(field == 2, force, own), "sec", [(2, 3), (3, 2)])
    part = jnp.where(
        field == 3, (force - mate) / NSUB, jnp.where(field == 2, mate - own, own)
    )
    flat = part.reshape(levels, block_cols)
    cut = (targets, levels, per_target)
    tiled = per_target % LANES == 0
    if tiled:
        outgoing = permute(flat, slot_list[None, :], cut)
    else:
        in_slots = permute(flat, slot_list[None, :], flat.shape)
        outgoing = in_slots.reshape(levels, targets, per_target).transpose(1, 0, 2)
    crm_moisture, outgoing = lax.optimization_barrier((crm_moisture, outgoing))
    arrived = lax.all_to_all(outgoing, ("sec", "lat"), split_axis=0, concat_axis=0, tiled=True)
    homeward = cloud_model(arrived, crm_moisture[0, :, :, 0, 0, :], sections)
    returned = lax.all_to_all(homeward, ("sec", "lat"), split_axis=0, concat_axis=0, tiled=True)
    if not tiled:
        returned = returned.transpose(1, 0, 2).reshape(levels, block_cols)
    rainfall = permute(returned, inverse_order(slot_list)[None, :], flat.shape)
    rainfall = rainfall.reshape(levels, band_rows, lon_block)
    share = jnp.where(
        field < 2, own * (-1.0 / NSUB), jnp.where(field == 2, jnp.float32(1), jnp.float32(-1))
    )
    fresh = own + (share * rainfall + force)

    regrouped = lax.all_to_all(fresh, "col", split_axis=0, concat_axis=0, tiled=True)
    owner_count = MMAX // lat_bands
    wave_table, _ = lax.optimization_barrier((wave_table, rainfall))
    owned_waves = lax.dynamic_slice_in_dim(
        wave_table, lax.axis_index("lat") * owner_count, owner_count
    )
    tables = legendre_tables(owned_waves, NLAT, lat_bands)
    regrouped, tables = lax.optimization_barrier((regrouped, tables))
    spectra = dft(regrouped, wave_table, lax.axis_size("col"), lat_bands)
    gathered = lax.all_to_all(spectra, "lat", split_axis=0, concat_axis=0, tiled=True)
    coeffs = contract_tables(gathered, tables)
    return (fresh[None, None], coeffs[None, None])


def solution(mesh):
    placed = (
        P(None, "sec", None, "lat", "col"),
        P(None, "sec", None, "lat", "col"),
        P(None, None, None, ("sec", "lat"), "col", None),
        P("col", "lat", None),
        P(),
    )
    return jax.shard_map(
        shards,
        mesh=mesh,
        in_specs=placed,
        out_specs=(P(None, "sec", None, "lat", "col"), P("sec", None, "col", "lat", None, None)),
        check_vma=False,
    )
```
